32 devices in a mesh: mem: 16 (over z, x, core), hist: 2 (over y).
Axes of the slice: x: 2, y: 2, z: 4, core: 2. Of those that a mesh axis runs over, the one named last changes fastest.
Arguments:
- memory_block: bfloat16 [64, 16, 64, 128], P('mem', 'hist'), may hold values from -1.5 to 1.5
- memory_rows: bfloat16 [32768, 2, 128], P(('mem', 'hist')), may hold values from -6 to 6
- panel_rows: bfloat16 [8192, 2, 128], P(('hist', 'mem')), may hold values from -6 to 6
- time_deal: int32 [64], replicated, may hold values from 0 to 63, each once
- column_times: int32 [16], replicated, may hold values from 0 to 63
- window_start: int32 [1], replicated, may hold values from 0 to 32
- coupling: float32 [64, 64], replicated, may hold values from -0.375 to 0.375
- hamiltonian: bfloat16 [64, 64], replicated, may hold values from -6 to 6
Outputs:
- new_rows: bfloat16 [8192, 2, 128], P(('hist', 'mem'))
- new_sigma: bfloat16 [8192, 2, 128], P(('hist', 'mem'))
The draws below stay inside these ranges and needn't reach their ends.
Inputs may be any that keep to these rules, and one draw needn't show every extreme that they name: `time_deal`: each of 0 to 63 once.
All inputs are finite; a program needn't handle non-finite values.
Results may differ from the reference program's by a relative error of at most 0.014.
Values may be sent and summed in bfloat16 or wider, within the bound.
No kernel may reach another device: no remote copies, remote signals or barrier semaphores. Data moves between devices by JAX's collectives and lax.ppermute only.
A program may use at most 64 MiB of HBM per device.

```python
import jax
import jax.numpy as jnp
from jax import lax

NO = 64
P_SIZE = 8
NPAN = 2
W = 64
C = 16


def place_ends(array, key, smallest, top_value):
    longest = array.shape.index(max(array.shape))
    spots = []
    for shift in (0, 1):
        where = [jax.random.randint(jax.random.fold_in(key, axis), (), 0, length) for axis, length in enumerate(array.shape)]
        where[longest] = (where[longest] + shift) % array.shape[longest]
        spots.append(tuple(where))
    return array.at[spots[0]].set(smallest).at[spots[1]].set(top_value)


def steps_of(stream_key, dims, split, smallest, top_value):
    level, own = 1.0, jax.random.fold_in(stream_key, 6)
    for axis_at, blocks in split:
        draws = jnp.exp(jax.random.uniform(jax.random.fold_in(own, axis_at), (blocks,), jnp.float32, smallest / len(split), top_value / len(split)))
        level = level * jnp.repeat(draws, dims[axis_at] // blocks).reshape([-1 if axis == axis_at else 1 for axis in range(len(dims))])
    return level


def centred(rng, extent, scale, most, pieces=(), kind=jnp.bfloat16):
    loudness = steps_of(rng, extent, pieces, -0.22, 0.18) if pieces else 1.0
    result = jax.random.normal(rng, extent, jnp.float32) * scale * loudness
    return jnp.minimum(jnp.maximum(result, -most), most).astype(kind)


def setup_inputs(seed: int = 0) -> dict:
    keys = jax.random.split(jax.random.key(seed), 9)
    memory_block = centred(keys[0], (W, C, NO, 2 * NO), 0.25, 1.5, ((0, 16), (1, 2)))
    memory_rows = centred(keys[1], (W * P_SIZE * NO, NPAN, 2 * NO), 1.0, 6.0, ((0, 32),))
    panel_rows = centred(keys[2], (C * P_SIZE * NO, NPAN, 2 * NO), 1.0, 6.0, ((0, 32),))
    time_deal = jax.random.permutation(keys[3], W).astype(jnp.int32)
    column_times = place_ends(jax.random.randint(keys[4], (C,), 0, W), jax.random.fold_in(keys[4], 1), 0, W - 1).astype(jnp.int32)
    window_start = jax.random.randint(keys[5], (1,), 0, W // 2 + 1).astype(jnp.int32)
    coupling = centred(keys[6], (NO, NO), (4 * NO) ** -0.5, 0.375, (), jnp.float32)
    hamiltonian = centred(keys[7], (NO, NO), 1.0, 6.0)
    return dict(memory_block=memory_block, memory_rows=memory_rows, panel_rows=panel_rows, time_deal=time_deal, column_times=column_times, window_start=window_start, coupling=coupling, hamiltonian=hamiltonian)


time_step = 0.02


def sigma_of(tiles, coupling):
    orbitals = coupling.shape[0]
    real_part = tiles[..., :orbitals]
    imag_part = tiles[..., orbitals:]
    bubble = real_part * real_part + imag_part * imag_part
    screened = jnp.einsum('ik,...kpl->...ipl', coupling, bubble, precision=lax.Precision.HIGHEST)
    screening = jnp.einsum('...ipl,jl->...ipj', screened, coupling, precision=lax.Precision.HIGHEST)
    return -jnp.concatenate([real_part * screening, imag_part * screening], -1)


def complex_form(tiles):
    orbitals = tiles.shape[-1] // 2
    real_part = tiles[..., :orbitals]
    imag_part = tiles[..., orbitals:]
    upper = jnp.concatenate([real_part, imag_part], -1)
    lower = jnp.concatenate([-imag_part, real_part], -1)
    return jnp.concatenate([upper, lower], -2)


def reference(memory_block, memory_rows, panel_rows, time_deal, column_times, window_start, coupling, hamiltonian):
    memory_tiles = memory_rows.reshape(W, P_SIZE, NO, NPAN, 2 * NO).astype(jnp.float32)
    old_sigma = sigma_of(memory_tiles, coupling).astype(jnp.bfloat16).astype(jnp.float32)
    causal = (time_deal[:, None] >= column_times[None, :]) & (time_deal[:, None] >= window_start[0])

    def column_term(operands):
        column_tiles, column_mask = operands
        block_form = complex_form(column_tiles.astype(jnp.float32)) * column_mask[:, None, None].astype(jnp.float32)
        return jnp.einsum('ktipr,krc->tipc', old_sigma, block_form)

    collision = lax.map(column_term, (jnp.swapaxes(memory_block, 0, 1), causal.T))
    panel_tiles = panel_rows.reshape(C, P_SIZE, NO, NPAN, 2 * NO).astype(jnp.float32)
    applied = jnp.einsum('ik,jtkpc->jtipc', hamiltonian.astype(jnp.float32), panel_tiles)
    turned = jnp.concatenate([applied[..., NO:], -applied[..., :NO]], -1)
    advanced = (panel_tiles + time_step * (turned + collision)).astype(jnp.bfloat16)
    new_sigma = sigma_of(advanced.astype(jnp.float32), coupling).astype(jnp.bfloat16)
    return advanced.reshape(C * P_SIZE * NO, NPAN, 2 * NO), new_sigma.reshape(C * P_SIZE * NO, NPAN, 2 * NO)
```

```python
import functools

import jax
import jax.numpy as jnp
from jax import lax
from jax.experimental import pallas as pl
from jax.experimental.pallas import tpu as pltpu
from jax.sharding import PartitionSpec as P

P_SIZE = 8
CHUNKS = 2


time_step = 0.02
F32 = jnp.float32
BF16 = jnp.bfloat16


def dot(left, right):
    return jnp.dot(left, right, preferred_element_type=F32)


def halves(value):
    top = value.astype(BF16)
    return top, (value - top.astype(F32)).astype(BF16)


def sigma_tiles(tiles, consts):
    n, rows, lanes = tiles.shape
    right_top, right_low, left_top, left_low = consts
    flat = tiles.reshape(n * rows, lanes).astype(F32)
    top, low = halves(flat * flat)
    screened = dot(top, right_top) + (dot(low, right_top) + dot(top, right_low))
    top, low = halves(screened)
    top, low = top.reshape(n, rows, lanes), low.reshape(n, rows, lanes)
    out = []
    step = 2 if n % 2 == 0 else 1
    for start in range(0, n, step):
        tops = jnp.concatenate([top[start + s] for s in range(step)], 1)
        lows = jnp.concatenate([low[start + s] for s in range(step)], 1)
        both = dot(left_top, tops) + (dot(left_top, lows) + dot(left_low, tops))
        for s in range(step):
            out.append(both[:, s * lanes:(s + 1) * lanes])
    screening = jnp.stack(out).reshape(n * rows, lanes)
    return (-flat * screening).reshape(n, rows, lanes)


def call(body, outs, *args, flops=0, **keywords):
    moved = sum(a.size * a.dtype.itemsize for a in list(args) + list(outs))
    return pl.pallas_call(
        body,
        out_shape=outs,
        cost_estimate=pl.CostEstimate(flops=flops, bytes_accessed=moved, transcendentals=0),
        **keywords,
    )(*args)


def shape(dims, kind):
    return jax.ShapeDtypeStruct(tuple(dims), kind)


def split_body(rows_ref, *outs):
    core = lax.axis_index("mem") & 1
    parts = len(outs) // 2
    for c in range(parts):
        size = outs[2 * c].shape[2]
        outs[2 * c][...] = rows_ref[:, :, core, c * size:(c + 1) * size]
        outs[2 * c + 1][...] = rows_ref[:, :, 1 - core, c * size:(c + 1) * size]


def early_body(n_early, slot_of, groups, chunks, deal_ref, columns_ref, start_ref, block_ref, other_ref, coupling_ref, ham_ref, panel_ref, *refs):
    early = refs[:n_early * chunks]
    weights_ref, consts_ref, base_ref = refs[n_early * chunks:n_early * chunks + 3]
    sigmas = refs[n_early * chunks + 3:]
    orbitals = coupling_ref.shape[0]
    rows = consts_ref.shape[1]
    panels = rows // orbitals
    mem, hist = lax.axis_index("mem"), lax.axis_index("hist")
    core, pair = mem & 1, mem >> 1
    slots, columns = block_ref.shape[0], block_ref.shape[1]

    spread = (lax.broadcasted_iota(jnp.int32, (rows, orbitals), 0) // panels == lax.broadcasted_iota(jnp.int32, (rows, orbitals), 1)).astype(F32)
    row_at = lax.broadcasted_iota(jnp.int32, (rows, rows), 0)
    lane_at = lax.broadcasted_iota(jnp.int32, (rows, rows), 1)
    same = (row_at % panels == lane_at % panels).astype(F32)

    def exact(left, right, dims):
        return lax.dot_general(left, right, (dims, ((), ())), precision=lax.Precision.HIGHEST, preferred_element_type=F32)

    def rowed(matrix):
        return exact(exact(spread, matrix, ((1,), (0,))), spread, ((1,), (1,))) * same

    lanes = 2 * orbitals
    fold = (lax.broadcasted_iota(jnp.int32, (lanes, orbitals), 0) % orbitals == lax.broadcasted_iota(jnp.int32, (lanes, orbitals), 1)).astype(F32)
    coupling = coupling_ref[...]
    right = exact(exact(fold, coupling, ((1,), (1,))), fold, ((1,), (1,)))
    right_top, right_low = halves(right)
    left_top, left_low = halves(rowed(coupling))
    for at, value in enumerate((right_top, right_low, left_top, left_low)):
        consts_ref[at] = value
    consts = (right_top, right_low, left_top, left_low)

    ham = rowed(ham_ref[...].astype(F32)).astype(BF16)
    sign = jnp.where(lax.broadcasted_iota(jnp.int32, (rows, lanes), 1) < orbitals, 1.0, -1.0).astype(F32)
    for tile in range(panel_ref.shape[0]):
        values = panel_ref[tile]
        turned = pltpu.roll(dot(ham, values), orbitals, 1) * sign
        base_ref[tile] = values.astype(F32) + time_step * turned

    for at in range(n_early * chunks):
        source = early[at]
        tiles = sigma_tiles(source[...].reshape((-1,) + source.shape[3:]), consts)
        sigmas[at][...] = tiles.astype(BF16).reshape(source.shape)

    flip = jnp.where(lax.broadcasted_iota(jnp.int32, (orbitals, lanes), 1) < orbitals, -1.0, 1.0).astype(F32)
    own_column = pair // groups
    begin = start_ref[0]
    for q in range(2 * slots):
        foreign, local = slot_of(q, hist)
        source = other_ref if foreign else block_ref
        mem_of = (mem ^ 1) if foreign else mem
        time = deal_ref[mem_of * slots + local]
        for apart in range(columns):
            column = own_column ^ apart
            keep = jnp.logical_and(time >= columns_ref[hist * columns + column], time >= begin)
            upper = source[local, column].astype(F32) * jnp.where(keep, 1.0, 0.0).astype(F32)
            lower = pltpu.roll(upper, orbitals, 1) * flip
            weights_ref[q * lanes:q * lanes + orbitals, apart * lanes:(apart + 1) * lanes] = upper.astype(BF16)
            weights_ref[q * lanes + orbitals:(q + 1) * lanes, apart * lanes:(apart + 1) * lanes] = lower.astype(BF16)


def term_body(n_done, n_late, order, groups, consts_ref, weights_ref, *refs):
    done, late = refs[:n_done], refs[n_done:n_done + n_late]
    send_ref, keep_ref, left_ref = refs[n_done + n_late:]
    pair = lax.axis_index("mem") >> 1
    own_group = pair % groups
    consts = tuple(consts_ref[at] for at in range(4))
    rows, lanes = send_ref.shape[1:]
    for step in range(groups):
        group = own_group ^ step
        q = 0
        for at, source in enumerate(done + late):
            tiles = source[:, group]
            count = tiles.shape[0]
            if at >= n_done:
                tiles = sigma_tiles(tiles.reshape((-1,) + tiles.shape[2:]), consts).astype(BF16).reshape(tiles.shape)
            for s in range(count):
                left_ref[:, q * lanes:(q + 1) * lanes] = tiles[s].reshape(rows, lanes)
                q += 1
        total = dot(left_ref[...], weights_ref[...])
        for place, block in enumerate(order):
            if block % groups != step:
                continue
            apart = block // groups
            value = total[:, apart * lanes:(apart + 1) * lanes]
            if place < len(order) // 2:
                send_ref[place] = value.astype(BF16)
            else:
                keep_ref[place - len(order) // 2] = value


def add_body(keep_ref, got_ref, send_ref, next_ref):
    half = send_ref.shape[0]
    send_ref[...] = (keep_ref[:half] + got_ref[:half].astype(F32)).astype(BF16)
    next_ref[...] = keep_ref[half:] + got_ref[half:].astype(F32)


def last_body(chunks, consts_ref, base_ref, *refs):
    keeps, gots = refs[:chunks], refs[chunks:2 * chunks]
    rows_ref, sigma_ref = refs[2 * chunks:]
    consts = tuple(consts_ref[at] for at in range(4))
    size = base_ref.shape[0] // chunks
    for c in range(chunks):
        here = slice(c * size, (c + 1) * size)
        collision = (keeps[c][...] + gots[c][...].astype(F32)).reshape((size,) + base_ref.shape[1:])
        rows = (base_ref[here] + time_step * collision).astype(BF16)
        rows_ref[here] = rows
        sigma_ref[here] = sigma_tiles(rows, consts).astype(BF16)


def block_order(count, masks):
    order = [0]
    for mask in reversed(masks):
        order = [block ^ mask for block in order] + order
    return order


def exchange(value, mem_mask, hist_mask):
    mems, hists = lax.axis_size("mem"), lax.axis_size("hist")
    pairs = [(m * hists + h, (m ^ mem_mask) * hists + (h ^ hist_mask)) for m in range(mems) for h in range(hists)]
    return lax.ppermute(value, ("mem", "hist"), pairs)


def local(memory_block, memory_rows, panel_rows, time_deal, column_times, window_start, coupling, hamiltonian):
    orbitals = coupling.shape[0]
    panels, lanes = panel_rows.shape[1:]
    rows = orbitals * panels
    slots = memory_block.shape[0]
    columns = memory_block.shape[1]
    pairs = lax.axis_size("mem") // 2
    own_tiles = panel_rows.shape[0] // orbitals
    groups = P_SIZE // (2 * own_tiles)
    chunks = CHUNKS if own_tiles % CHUNKS == 0 else 1
    part = own_tiles // chunks
    two_hist = lax.axis_size("hist") == 2

    if not two_hist:
        memory_rows = lax.all_gather(memory_rows, "hist", axis=0, tiled=True)
    held = memory_rows.shape[0] // (P_SIZE * orbitals)
    tiles = memory_rows.reshape(held, groups, 2, own_tiles, rows, lanes)
    panel_tiles = panel_rows.reshape(own_tiles, rows, lanes)
    piece = shape((held, groups, part, rows, lanes), BF16)
    split = call(split_body, [piece] * (2 * chunks), tiles)
    mine, other = split[0::2], split[1::2]

    if two_hist:
        same_core = [exchange(mine[c], 0, 1) for c in range(chunks)]
        cross = [exchange(other[c], 1, 1) for c in range(chunks)]
    partner_block = exchange(memory_block, 1, 0)
    partner = [exchange(other[c], 1, 0) for c in range(chunks)]

    if two_hist:
        def slot_of(q, hist):
            return (q // held) % 2, (hist ^ (q // (2 * held))) * held + q % held
    else:
        def slot_of(q, hist):
            return q // held, q % held

    early = [mine, partner]
    n_early = len(early)
    flat_early = [array for source in early for array in source]
    smem = pl.BlockSpec(memory_space=pltpu.SMEM)
    vmem = pl.BlockSpec(memory_space=pltpu.VMEM)
    outs = [
        shape((2 * slots * lanes, columns * lanes), BF16),
        shape((4, rows, lanes), BF16),
        shape((own_tiles, rows, lanes), F32),
    ] + [piece] * (n_early * chunks)
    weights, consts, base, *sigmas = call(
        functools.partial(early_body, n_early, slot_of, groups, chunks),
        outs,
        time_deal, column_times, window_start, memory_block, partner_block, coupling, hamiltonian, panel_tiles, *flat_early,
        in_specs=[smem] * 3 + [vmem] * (5 + n_early * chunks),
    )

    bits = [1 << b for b in range(pairs.bit_length() - 1)]
    if len(bits) > 1:
        bits[-1] |= bits[-2]
    finals = []
    for c in range(chunks):
        masks = list(bits)
        order = block_order(pairs, masks)
        height = part * rows
        done = [sigmas[e * chunks + c] for e in range(n_early)]
        late = [same_core[c], cross[c]] if two_hist else []
        send, keep = call(
            functools.partial(term_body, len(done), len(late), order, groups),
            [shape((pairs // 2, height, lanes), BF16), shape((pairs // 2, height, lanes), F32)],
            consts, weights, *done, *late,
            flops=2 * height * groups * 2 * slots * lanes * columns * lanes,
            scratch_shapes=[pltpu.VMEM((height, 2 * slots * lanes), BF16)],
        )
        for at, mask in enumerate(masks):
            got = exchange(send, 2 * mask, 0)
            if at + 1 < len(masks):
                half = keep.shape[0] // 2
                send, keep = call(
                    add_body,
                    [shape((half, height, lanes), BF16), shape((half, height, lanes), F32)],
                    keep, got,
                )
        finals.append((keep, got))

    result = shape((own_tiles, rows, lanes), BF16)
    new_rows, new_sigma = call(
        functools.partial(last_body, chunks),
        [result, result],
        consts, base, *[keep for keep, _ in finals], *[got for _, got in finals],
    )
    return new_rows.reshape(panel_rows.shape), new_sigma.reshape(panel_rows.shape)


def solution(mesh):
    in_specs = (
        P("mem", "hist", None, None),
        P(("mem", "hist"), None, None),
        P(("hist", "mem"), None, None),
        P(),
        P(),
        P(),
        P(),
        P(),
    )
    out_specs = (P(("hist", "mem"), None, None), P(("hist", "mem"), None, None))
    return jax.shard_map(local, mesh=mesh, in_specs=in_specs, out_specs=out_specs, check_vma=False)
```

```python
import functools

import jax
import jax.numpy as jnp
from jax import lax
from jax.experimental import pallas as pl
from jax.experimental.pallas import tpu as pltpu
from jax.sharding import PartitionSpec as P

P_SIZE = 8
CHUNKS = 2


time_step = 0.02
F32 = jnp.float32
BF16 = jnp.bfloat16


def dot(left, right):
    return jnp.dot(left, right, preferred_element_type=F32)


def halves(value):
    top = value.astype(BF16)
    return top, (value - top.astype(F32)).astype(BF16)


def sigma_tiles(tiles, consts):
    n, rows, lanes = tiles.shape
    right_top, right_low, left_top, left_low = consts
    flat = tiles.reshape(n * rows, lanes).astype(F32)
    top, low = halves(flat * flat)
    screened = dot(top, right_top) + (dot(low, right_top) + dot(top, right_low))
    top, low = halves(screened)
    top, low = top.reshape(n, rows, lanes), low.reshape(n, rows, lanes)
    out = []
    step = 2 if n % 2 == 0 else 1
    for start in range(0, n, step):
        tops = jnp.concatenate([top[start + s] for s in range(step)], 1)
        lows = jnp.concatenate([low[start + s] for s in range(step)], 1)
        both = dot(left_top, tops) + (dot(left_top, lows) + dot(left_low, tops))
        for s in range(step):
            out.append(both[:, s * lanes:(s + 1) * lanes])
    screening = jnp.stack(out).reshape(n * rows, lanes)
    return (-flat * screening).reshape(n, rows, lanes)


def call(body, outs, *args, flops=0, **keywords):
    moved = sum(a.size * a.dtype.itemsize for a in list(args) + list(outs))
    return pl.pallas_call(
        body,
        out_shape=outs,
        cost_estimate=pl.CostEstimate(flops=flops, bytes_accessed=moved, transcendentals=0),
        compiler_params=pltpu.CompilerParams(vmem_limit_bytes=16 << 20),
        **keywords,
    )(*args)


def shape(dims, kind):
    return jax.ShapeDtypeStruct(tuple(dims), kind)


def split_body(rows_ref, *outs):
    core = lax.axis_index("mem") & 1
    parts = len(outs) // 2
    for c in range(parts):
        size = outs[2 * c].shape[2]
        outs[2 * c][...] = rows_ref[:, :, core, c * size:(c + 1) * size]
        outs[2 * c + 1][...] = rows_ref[:, :, 1 - core, c * size:(c + 1) * size]


def early_body(n_early, slot_of, groups, chunks, deal_ref, columns_ref, start_ref, block_ref, other_ref, coupling_ref, ham_ref, panel_ref, *refs):
    early = refs[:n_early * chunks]
    weights_ref, consts_ref, base_ref = refs[n_early * chunks:n_early * chunks + 3]
    sigmas = refs[n_early * chunks + 3:]
    orbitals = coupling_ref.shape[0]
    rows = consts_ref.shape[1]
    panels = rows // orbitals
    mem, hist = lax.axis_index("mem"), lax.axis_index("hist")
    core, pair = mem & 1, mem >> 1
    slots, columns = block_ref.shape[0], block_ref.shape[1]

    spread = (lax.broadcasted_iota(jnp.int32, (rows, orbitals), 0) // panels == lax.broadcasted_iota(jnp.int32, (rows, orbitals), 1)).astype(F32)
    row_at = lax.broadcasted_iota(jnp.int32, (rows, rows), 0)
    lane_at = lax.broadcasted_iota(jnp.int32, (rows, rows), 1)
    same = (row_at % panels == lane_at % panels).astype(F32)

    def exact(left, right, dims):
        return lax.dot_general(left, right, (dims, ((), ())), precision=lax.Precision.HIGHEST, preferred_element_type=F32)

    def rowed(matrix):
        return exact(exact(spread, matrix, ((1,), (0,))), spread, ((1,), (1,))) * same

    lanes = 2 * orbitals
    fold = (lax.broadcasted_iota(jnp.int32, (lanes, orbitals), 0) % orbitals == lax.broadcasted_iota(jnp.int32, (lanes, orbitals), 1)).astype(F32)
    coupling = coupling_ref[...]
    right = exact(exact(fold, coupling, ((1,), (1,))), fold, ((1,), (1,)))
    right_top, right_low = halves(right)
    left_top, left_low = halves(rowed(coupling))
    for at, value in enumerate((right_top, right_low, left_top, left_low)):
        consts_ref[at] = value
    consts = (right_top, right_low, left_top, left_low)

    ham = rowed(ham_ref[...].astype(F32)).astype(BF16)
    sign = jnp.where(lax.broadcasted_iota(jnp.int32, (rows, lanes), 1) < orbitals, 1.0, -1.0).astype(F32)
    for tile in range(panel_ref.shape[0]):
        values = panel_ref[tile]
        turned = pltpu.roll(dot(ham, values), orbitals, 1) * sign
        base_ref[tile] = values.astype(F32) + time_step * turned

    for at in range(n_early * chunks):
        source = early[at]
        tiles = sigma_tiles(source[...].reshape((-1,) + source.shape[3:]), consts)
        sigmas[at][...] = tiles.astype(BF16).reshape(source.shape)

    flip = jnp.where(lax.broadcasted_iota(jnp.int32, (orbitals, lanes), 1) < orbitals, -1.0, 1.0).astype(F32)
    own_column = pair // groups
    begin = start_ref[0]
    for q in range(2 * slots):
        foreign, local = slot_of(q, hist)
        source = other_ref if foreign else block_ref
        mem_of = (mem ^ 1) if foreign else mem
        time = deal_ref[mem_of * slots + local]
        for apart in range(columns):
            column = own_column ^ apart
            keep = jnp.logical_and(time >= columns_ref[hist * columns + column], time >= begin)
            upper = source[local, column].astype(F32) * jnp.where(keep, 1.0, 0.0).astype(F32)
            lower = pltpu.roll(upper, orbitals, 1) * flip
            weights_ref[q * lanes:q * lanes + orbitals, apart * lanes:(apart + 1) * lanes] = upper.astype(BF16)
            weights_ref[q * lanes + orbitals:(q + 1) * lanes, apart * lanes:(apart + 1) * lanes] = lower.astype(BF16)


def term_body(n_done, n_late, order, groups, consts_ref, weights_ref, *refs):
    done, late = refs[:n_done], refs[n_done:n_done + n_late]
    send_ref, keep_ref, left_ref = refs[n_done + n_late:]
    pair = lax.axis_index("mem") >> 1
    own_group = pair % groups
    consts = tuple(consts_ref[at] for at in range(4))
    rows, lanes = send_ref.shape[1:]
    for step in range(groups):
        group = own_group ^ step
        q = 0
        for at, source in enumerate(done + late):
            tiles = source[:, group]
            count = tiles.shape[0]
            if at >= n_done:
                tiles = sigma_tiles(tiles.reshape((-1,) + tiles.shape[2:]), consts).astype(BF16).reshape(tiles.shape)
            for s in range(count):
                left_ref[:, q * lanes:(q + 1) * lanes] = tiles[s].reshape(rows, lanes)
                q += 1
        total = dot(left_ref[...], weights_ref[...])
        for place, block in enumerate(order):
            if block % groups != step:
                continue
            apart = block // groups
            value = total[:, apart * lanes:(apart + 1) * lanes]
            if place < len(order) // 2:
                send_ref[place] = value.astype(BF16)
            else:
                keep_ref[place - len(order) // 2] = value


def add_body(keep_ref, got_ref, send_ref, next_ref):
    half = send_ref.shape[0]
    send_ref[...] = (keep_ref[:half] + got_ref[:half].astype(F32)).astype(BF16)
    next_ref[...] = keep_ref[half:] + got_ref[half:].astype(F32)


def last_body(chunks, consts_ref, base_ref, *refs):
    keeps, gots = refs[:chunks], refs[chunks:2 * chunks]
    rows_ref, sigma_ref = refs[2 * chunks:]
    consts = tuple(consts_ref[at] for at in range(4))
    size = base_ref.shape[0] // chunks
    for c in range(chunks):
        here = slice(c * size, (c + 1) * size)
        collision = (keeps[c][...] + gots[c][...].astype(F32)).reshape((size,) + base_ref.shape[1:])
        rows = (base_ref[here] + time_step * collision).astype(BF16)
        rows_ref[here] = rows
        sigma_ref[here] = sigma_tiles(rows, consts).astype(BF16)


def block_order(count, masks):
    order = [0]
    for mask in reversed(masks):
        order = [block ^ mask for block in order] + order
    return order


def exchange(value, mem_mask, hist_mask):
    mems, hists = lax.axis_size("mem"), lax.axis_size("hist")
    pairs = [(m * hists + h, (m ^ mem_mask) * hists + (h ^ hist_mask)) for m in range(mems) for h in range(hists)]
    return lax.ppermute(value, ("mem", "hist"), pairs)


def local(memory_block, memory_rows, panel_rows, time_deal, column_times, window_start, coupling, hamiltonian):
    orbitals = coupling.shape[0]
    panels, lanes = panel_rows.shape[1:]
    rows = orbitals * panels
    slots = memory_block.shape[0]
    columns = memory_block.shape[1]
    pairs = lax.axis_size("mem") // 2
    own_tiles = panel_rows.shape[0] // orbitals
    groups = P_SIZE // (2 * own_tiles)
    chunks = CHUNKS if own_tiles % CHUNKS == 0 else 1
    part = own_tiles // chunks
    two_hist = lax.axis_size("hist") == 2

    if not two_hist:
        memory_rows = lax.all_gather(memory_rows, "hist", axis=0, tiled=True)
    held = memory_rows.shape[0] // (P_SIZE * orbitals)
    tiles = memory_rows.reshape(held, groups, 2, own_tiles, rows, lanes)
    panel_tiles = panel_rows.reshape(own_tiles, rows, lanes)
    piece = shape((held, groups, part, rows, lanes), BF16)
    split = call(split_body, [piece] * (2 * chunks), tiles)
    mine, other = split[0::2], split[1::2]

    if two_hist:
        same_core = [exchange(mine[c], 0, 1) for c in range(chunks)]
        cross = [exchange(other[c], 1, 1) for c in range(chunks)]
    partner_block = exchange(memory_block, 1, 0)
    partner = [exchange(other[c], 1, 0) for c in range(chunks)]

    if two_hist:
        def slot_of(q, hist):
            return (q // held) % 2, (hist ^ (q // (2 * held))) * held + q % held
    else:
        def slot_of(q, hist):
            return q // held, q % held

    early = [mine, partner]
    n_early = len(early)
    flat_early = [array for source in early for array in source]
    smem = pl.BlockSpec(memory_space=pltpu.SMEM)
    vmem = pl.BlockSpec(memory_space=pltpu.VMEM)
    outs = [
        shape((2 * slots * lanes, columns * lanes), BF16),
        shape((4, rows, lanes), BF16),
        shape((own_tiles, rows, lanes), F32),
    ] + [piece] * (n_early * chunks)
    weights, consts, base, *sigmas = call(
        functools.partial(early_body, n_early, slot_of, groups, chunks),
        outs,
        time_deal, column_times, window_start, memory_block, partner_block, coupling, hamiltonian, panel_tiles, *flat_early,
        in_specs=[smem] * 3 + [vmem] * (5 + n_early * chunks),
    )

    bits = [1 << b for b in range(pairs.bit_length() - 1)]
    if len(bits) > 1:
        bits[-1] |= bits[-2]
    finals = []
    for c in range(chunks):
        masks = list(bits)
        order = block_order(pairs, masks)
        height = part * rows
        done = [sigmas[e * chunks + c] for e in range(n_early)]
        late = [same_core[c], cross[c]] if two_hist else []
        send, keep = call(
            functools.partial(term_body, len(done), len(late), order, groups),
            [shape((pairs // 2, height, lanes), BF16), shape((pairs // 2, height, lanes), F32)],
            consts, weights, *done, *late,
            flops=2 * height * groups * 2 * slots * lanes * columns * lanes,
            scratch_shapes=[pltpu.VMEM((height, 2 * slots * lanes), BF16)],
        )
        for at, mask in enumerate(masks):
            got = exchange(send, 2 * mask, 0)
            if at + 1 < len(masks):
                half = keep.shape[0] // 2
                send, keep = call(
                    add_body,
                    [shape((half, height, lanes), BF16), shape((half, height, lanes), F32)],
                    keep, got,
                )
        finals.append((keep, got))

    result = shape((own_tiles, rows, lanes), BF16)
    new_rows, new_sigma = call(
        functools.partial(last_body, chunks),
        [result, result],
        consts, base, *[keep for keep, _ in finals], *[got for _, got in finals],
    )
    return new_rows.reshape(panel_rows.shape), new_sigma.reshape(panel_rows.shape)


def solution(mesh):
    in_specs = (
        P("mem", "hist", None, None),
        P(("mem", "hist"), None, None),
        P(("hist", "mem"), None, None),
        P(),
        P(),
        P(),
        P(),
        P(),
    )
    out_specs = (P(("hist", "mem"), None, None), P(("hist", "mem"), None, None))
    return jax.shard_map(local, mesh=mesh, in_specs=in_specs, out_specs=out_specs, check_vma=False)
```

```python
import functools

import jax
import jax.numpy as jnp
from jax import lax
from jax.experimental import pallas as pl
from jax.experimental.pallas import tpu as pltpu
from jax.sharding import PartitionSpec as P


P_SIZE = 8
CHUNKS = 2
PREFETCH_FLOPS = 2_000_000_000


time_step = 0.02
F32 = jnp.float32
BF16 = jnp.bfloat16


def dot(left, right):
    return jnp.dot(left, right, preferred_element_type=F32)


def halves(value):
    top = value.astype(BF16)
    return top, (value - top.astype(F32)).astype(BF16)


def sigma_tiles(tiles, consts):
    n, rows, lanes = tiles.shape
    right_top, right_low, left_top, left_low = consts
    flat = tiles.reshape(n * rows, lanes).astype(F32)
    top, low = halves(flat * flat)
    screened = dot(top, right_top) + (dot(low, right_top) + dot(top, right_low))
    top, low = halves(screened)
    top, low = top.reshape(n, rows, lanes), low.reshape(n, rows, lanes)
    out = []
    step = 2 if n % 2 == 0 else 1
    for start in range(0, n, step):
        tops = jnp.concatenate([top[start + s] for s in range(step)], 1)
        lows = jnp.concatenate([low[start + s] for s in range(step)], 1)
        both = dot(left_top, tops) + (dot(left_top, lows) + dot(left_low, tops))
        for s in range(step):
            out.append(both[:, s * lanes:(s + 1) * lanes])
    screening = jnp.stack(out).reshape(n * rows, lanes)
    return (-flat * screening).reshape(n, rows, lanes)


def call(body, outs, *args, flops=0, grant=16, **keywords):
    moved = sum(a.size * a.dtype.itemsize for a in list(args) + list(outs))
    return pl.pallas_call(
        body,
        out_shape=outs,
        cost_estimate=pl.CostEstimate(flops=flops, bytes_accessed=moved, transcendentals=0),
        compiler_params=pltpu.CompilerParams(vmem_limit_bytes=grant << 20),
        **keywords,
    )(*args)


def shape(dims, kind):
    return jax.ShapeDtypeStruct(tuple(dims), kind)


def split_body(rows_ref, *refs):
    core = lax.axis_index("mem") & 1
    outs, sems = refs[:-1], refs[-1]
    copies = []
    for at, out in enumerate(outs):
        size = out.shape[2]
        first = (at // 2) * size
        half = core if at % 2 == 0 else 1 - core
        copies.append(pltpu.make_async_copy(rows_ref.at[:, :, half, first:first + size], out, sems.at[at]))
    for copy in copies:
        copy.start()
    for copy in copies:
        copy.wait()


def early_body(n_early, slot_of, groups, chunks, deal_ref, columns_ref, start_ref, coupling_ref, ham_ref, panel_ref, block_ref, other_ref, *refs):
    early = refs[:n_early * chunks]
    weights_ref, consts_ref, base_ref = refs[n_early * chunks:n_early * chunks + 3]
    sigmas = refs[n_early * chunks + 3:]
    orbitals = coupling_ref.shape[0]
    rows = consts_ref.shape[1]
    panels = rows // orbitals
    mem, hist = lax.axis_index("mem"), lax.axis_index("hist")
    pair = mem >> 1
    slots, columns = block_ref.shape[0], block_ref.shape[1]

    spread = (lax.broadcasted_iota(jnp.int32, (rows, orbitals), 0) // panels == lax.broadcasted_iota(jnp.int32, (rows, orbitals), 1)).astype(F32)
    row_at = lax.broadcasted_iota(jnp.int32, (rows, rows), 0)
    lane_at = lax.broadcasted_iota(jnp.int32, (rows, rows), 1)
    same = (row_at % panels == lane_at % panels).astype(F32)

    def exact(left, right, dims):
        return lax.dot_general(left, right, (dims, ((), ())), precision=lax.Precision.HIGHEST, preferred_element_type=F32)

    def rowed(matrix):
        return exact(exact(spread, matrix, ((1,), (0,))), spread, ((1,), (1,))) * same

    lanes = 2 * orbitals
    fold = (lax.broadcasted_iota(jnp.int32, (lanes, orbitals), 0) % orbitals == lax.broadcasted_iota(jnp.int32, (lanes, orbitals), 1)).astype(F32)
    coupling = coupling_ref[...]
    right = exact(exact(fold, coupling, ((1,), (1,))), fold, ((1,), (1,)))
    right_top, right_low = halves(right)
    left_top, left_low = halves(rowed(coupling))
    for at, value in enumerate((right_top, right_low, left_top, left_low)):
        consts_ref[at] = value
    consts = (right_top, right_low, left_top, left_low)

    for at in range(n_early * chunks):
        source = early[at]
        tiles = sigma_tiles(source[...].reshape((-1,) + source.shape[3:]), consts)
        sigmas[at][...] = tiles.astype(BF16).reshape(source.shape)

    ham = rowed(ham_ref[...].astype(F32)).astype(BF16)
    sign = jnp.where(lax.broadcasted_iota(jnp.int32, (rows, lanes), 1) < orbitals, 1.0, -1.0).astype(F32)
    for tile in range(panel_ref.shape[0]):
        values = panel_ref[tile]
        turned = pltpu.roll(dot(ham, values), orbitals, 1) * sign
        base_ref[tile] = values.astype(F32) + time_step * turned

    flip = jnp.where(lax.broadcasted_iota(jnp.int32, (orbitals, lanes), 1) < orbitals, -1.0, 1.0).astype(F32)
    own_column = pair // groups
    begin = start_ref[0]
    for q in range(2 * slots):
        foreign, local = slot_of(q, hist)
        source = other_ref if foreign else block_ref
        mem_of = (mem ^ 1) if foreign else mem
        time = deal_ref[mem_of * slots + local]
        for apart in range(columns):
            column = own_column ^ apart
            keep = jnp.logical_and(time >= columns_ref[hist * columns + column], time >= begin)
            upper = source[local, column].astype(F32) * jnp.where(keep, 1.0, 0.0).astype(F32)
            lower = pltpu.roll(upper, orbitals, 1) * flip
            weights_ref[q * lanes:q * lanes + orbitals, apart * lanes:(apart + 1) * lanes] = upper.astype(BF16)
            weights_ref[q * lanes + orbitals:(q + 1) * lanes, apart * lanes:(apart + 1) * lanes] = lower.astype(BF16)


def term_body(n_done, n_late, places, groups, consts_ref, weights_ref, *refs):
    done, late = refs[:n_done], refs[n_done:n_done + n_late]
    outs, left_ref = refs[n_done + n_late:-1], refs[-1]
    pair = lax.axis_index("mem") >> 1
    own_group = pair % groups
    consts = tuple(consts_ref[at] for at in range(4))
    rows, lanes = outs[0].shape[1:]
    for step in range(groups):
        group = own_group ^ step
        q = 0
        for at, source in enumerate(done + late):
            tiles = source[:, group]
            count = tiles.shape[0]
            if at >= n_done:
                tiles = sigma_tiles(tiles.reshape((-1,) + tiles.shape[2:]), consts).astype(BF16).reshape(tiles.shape)
            for s in range(count):
                left_ref[:, q * lanes:(q + 1) * lanes] = tiles[s].reshape(rows, lanes)
                q += 1
        total = dot(left_ref[...], weights_ref[...])
        for block, (to, place) in places.items():
            if block % groups == step:
                apart = block // groups
                value = total[:, apart * lanes:(apart + 1) * lanes]
                outs[to][place] = value.astype(outs[to].dtype)


def add_body(n_got, keep_ref, *refs):
    gots, outs = refs[:n_got], refs[n_got:]
    total = keep_ref[...]
    for got in gots:
        total = total + got[...].astype(F32)
    size = outs[0].shape[0]
    for at, out in enumerate(outs):
        out[...] = total[at * size:(at + 1) * size].astype(out.dtype)


def last_body(chunks, n_got, consts_ref, base_ref, *refs):
    keeps, gots = refs[:chunks], refs[chunks:chunks + chunks * n_got]
    rows_ref, sigma_ref = refs[chunks + chunks * n_got:]
    consts = tuple(consts_ref[at] for at in range(4))
    size = base_ref.shape[0] // chunks
    for c in range(chunks):
        here = slice(c * size, (c + 1) * size)
        collision = keeps[c][...]
        for got in gots[c * n_got:(c + 1) * n_got]:
            collision = collision + got[...].astype(F32)
        collision = collision.reshape((size,) + base_ref.shape[1:])
        rows = (base_ref[here] + time_step * collision).astype(BF16)
        rows_ref[here] = rows
        sigma_ref[here] = sigma_tiles(rows, consts).astype(BF16)


def step_masks(count):
    bits = [1 << b for b in range(count.bit_length() - 1)]
    steps = []
    while bits:
        take = 1 if len(bits) % 2 else 2
        here, bits = bits[:take], bits[take:]
        masks = [0]
        for bit in here:
            masks = masks + [mask ^ bit for mask in masks]
        steps.append(masks[2:] + masks[1:2] + [0] if take == 2 else masks[::-1])
    return steps


def block_places(steps, parts):
    def spread(rest):
        if not rest:
            return [0]
        inner = spread(rest[1:])
        return [mask ^ block for mask in rest[0] for block in inner]

    inner = spread(steps[1:])
    size = len(inner) // parts
    return {mask ^ block: (place // size * len(steps[0]) + to, place % size) for to, mask in enumerate(steps[0]) for place, block in enumerate(inner)}


def exchange(value, mem_mask, hist_mask):
    mems, hists = lax.axis_size("mem"), lax.axis_size("hist")
    pairs = [(m * hists + h, (m ^ mem_mask) * hists + (h ^ hist_mask)) for m in range(mems) for h in range(hists)]
    return lax.ppermute(value, ("mem", "hist"), pairs)


def local(memory_block, memory_rows, panel_rows, time_deal, column_times, window_start, coupling, hamiltonian):
    orbitals = coupling.shape[0]
    panels, lanes = panel_rows.shape[1:]
    rows = orbitals * panels
    slots = memory_block.shape[0]
    columns = memory_block.shape[1]
    pairs = lax.axis_size("mem") // 2
    own_tiles = panel_rows.shape[0] // orbitals
    groups = P_SIZE // (2 * own_tiles)
    chunks = CHUNKS if own_tiles % CHUNKS == 0 else 1
    part = own_tiles // chunks
    two_hist = lax.axis_size("hist") == 2

    if not two_hist:
        memory_rows = lax.all_gather(memory_rows, "hist", axis=0, tiled=True)
    held = memory_rows.shape[0] // (P_SIZE * orbitals)
    tiles = memory_rows.reshape(held, groups, 2, own_tiles, rows, lanes)
    panel_tiles = panel_rows.reshape(own_tiles, rows, lanes)
    piece = shape((held, groups, part, rows, lanes), BF16)
    hbm = pl.BlockSpec(memory_space=pltpu.HBM)
    smem = pl.BlockSpec(memory_space=pltpu.SMEM)
    vmem = pl.BlockSpec(memory_space=pltpu.VMEM)
    split = call(
        split_body,
        [piece] * (2 * chunks),
        tiles,
        in_specs=[hbm],
        flops=PREFETCH_FLOPS,
        scratch_shapes=[pltpu.SemaphoreType.DMA((2 * chunks,))],
    )
    mine, other = split[0::2], split[1::2]

    if two_hist:
        same_core = [exchange(mine[c], 0, 1) for c in range(chunks)]
        cross = [exchange(other[c], 1, 1) for c in range(chunks)]
    partner_block = exchange(memory_block, 1, 0)
    partner = [exchange(other[c], 1, 0) for c in range(chunks)]

    if two_hist:
        def slot_of(q, hist):
            return (q // held) % 2, (hist ^ (q // (2 * held))) * held + q % held
    else:
        def slot_of(q, hist):
            return q // held, q % held

    early = [mine, partner]
    n_early = len(early)
    flat_early = [array for source in early for array in source]
    outs = [
        shape((2 * slots * lanes, columns * lanes), BF16),
        shape((4, rows, lanes), BF16),
        shape((own_tiles, rows, lanes), F32),
    ] + [piece] * (n_early * chunks)
    weights, consts, base, *sigmas = call(
        functools.partial(early_body, n_early, slot_of, groups, chunks),
        outs,
        time_deal, column_times, window_start, coupling, hamiltonian, panel_tiles, memory_block, partner_block, *flat_early,
        in_specs=[smem] * 3 + [vmem] * (5 + n_early * chunks),
    )

    steps = step_masks(pairs)
    parts = 2 if len(steps) > 1 else 1
    keeps, received = [], []
    for c in range(chunks):
        height = part * rows
        done = [sigmas[e * chunks + c] for e in range(n_early)]
        late = [same_core[c], cross[c]] if two_hist else []
        count = pairs // len(steps[0]) // parts

        def pieces(masks, count):
            return [shape((count, height, lanes), BF16 if mask else F32) for mask in masks]

        outs = call(
            functools.partial(term_body, len(done), len(late), block_places(steps, parts), groups),
            pieces(steps[0], count) * parts,
            consts, weights, *done, *late,
            flops=2 * height * groups * 2 * slots * lanes * columns * lanes,
            scratch_shapes=[pltpu.VMEM((height, 2 * slots * lanes), BF16)],
        )
        size = len(steps[0])
        state = [(outs[p * size:(p + 1) * size - 1], outs[(p + 1) * size - 1]) for p in range(parts)]
        for at, masks in enumerate(steps):
            gots = [[exchange(sends[i], 2 * masks[i], 0) for i in range(len(sends))] for sends, _ in state]
            if at + 1 == len(steps):
                break
            after = steps[at + 1]
            share = len(after) // len(state)
            count = count * len(state) // len(after)
            outs = []
            for p, (_, keep) in enumerate(state):
                outs += call(functools.partial(add_body, len(gots[p])), pieces(after[p * share:(p + 1) * share], count), keep, *gots[p])
            state = [(outs[:-1], outs[-1])]
        keeps.append(state[0][1])
        received += gots[0]

    result = shape((own_tiles, rows, lanes), BF16)
    new_rows, new_sigma = call(
        functools.partial(last_body, chunks, len(received) // chunks),
        [result, result],
        consts, base, *keeps, *received,
    )
    return new_rows.reshape(panel_rows.shape), new_sigma.reshape(panel_rows.shape)


def solution(mesh):
    in_specs = (
        P("mem", "hist", None, None),
        P(("mem", "hist"), None, None),
        P(("hist", "mem"), None, None),
        P(),
        P(),
        P(),
        P(),
        P(),
    )
    out_specs = (P(("hist", "mem"), None, None), P(("hist", "mem"), None, None))
    return jax.shard_map(local, mesh=mesh, in_specs=in_specs, out_specs=out_specs, check_vma=False)
```

```python
import functools

import jax
import jax.numpy as jnp
from jax import lax
from jax.experimental import pallas as pl
from jax.experimental.pallas import tpu as pltpu
from jax.sharding import PartitionSpec as P


P_SIZE = 8
CHUNKS = 2
PREFETCH_FLOPS = 2_000_000_000


time_step = 0.02
F32 = jnp.float32
BF16 = jnp.bfloat16


def dot(left, right):
    return jnp.dot(left, right, preferred_element_type=F32)


def halves(value):
    top = value.astype(BF16)
    return top, (value - top.astype(F32)).astype(BF16)


def sigma_tiles(tiles, consts):
    n, rows, lanes = tiles.shape
    right_top, right_low, left_top, left_low = consts
    flat = tiles.reshape(n * rows, lanes).astype(F32)
    top, low = halves(flat * flat)
    screened = dot(top, right_top) + (dot(low, right_top) + dot(top, right_low))
    top, low = halves(screened)
    top, low = top.reshape(n, rows, lanes), low.reshape(n, rows, lanes)
    out = []
    step = 2 if n % 2 == 0 else 1
    for start in range(0, n, step):
        tops = jnp.concatenate([top[start + s] for s in range(step)], 1)
        lows = jnp.concatenate([low[start + s] for s in range(step)], 1)
        both = dot(left_top, tops) + (dot(left_top, lows) + dot(left_low, tops))
        for s in range(step):
            out.append(both[:, s * lanes:(s + 1) * lanes])
    screening = jnp.stack(out).reshape(n * rows, lanes)
    return (-flat * screening).reshape(n, rows, lanes)


def call(body, outs, *args, flops=0, grant=16, **keywords):
    moved = sum(a.size * a.dtype.itemsize for a in list(args) + list(outs))
    return pl.pallas_call(
        body,
        out_shape=outs,
        cost_estimate=pl.CostEstimate(flops=flops, bytes_accessed=moved, transcendentals=0),
        compiler_params=pltpu.CompilerParams(vmem_limit_bytes=grant << 20),
        **keywords,
    )(*args)


def shape(dims, kind):
    return jax.ShapeDtypeStruct(tuple(dims), kind)


def split_body(rows_ref, *outs):
    core = lax.axis_index("mem") & 1
    for at, out in enumerate(outs):
        size = out.shape[2]
        first = (at // 2) * size
        out[...] = rows_ref[:, :, core if at % 2 == 0 else 1 - core, first:first + size]


def ready_body(count, coupling_ref, *refs):
    sources, consts_ref, sigmas = refs[:count], refs[count], refs[count + 1:]
    orbitals = coupling_ref.shape[0]
    lanes = 2 * orbitals
    fold = (lax.broadcasted_iota(jnp.int32, (lanes, orbitals), 0) % orbitals == lax.broadcasted_iota(jnp.int32, (lanes, orbitals), 1)).astype(F32)
    coupling = coupling_ref[...]
    right = exact(exact(fold, coupling, ((1,), (1,))), fold, ((1,), (1,)))
    consts = (*halves(right), *halves(row_matrix(coupling, consts_ref.shape[1])))
    for at, value in enumerate(consts):
        consts_ref[at] = value
    for source, sigma in zip(sources, sigmas):
        tiles = sigma_tiles(source[...].reshape((-1,) + source.shape[3:]), consts)
        sigma[...] = tiles.astype(BF16).reshape(source.shape)


def exact(left, right, dims):
    return lax.dot_general(left, right, (dims, ((), ())), precision=lax.Precision.HIGHEST, preferred_element_type=F32)


def row_matrix(matrix, rows):
    orbitals = matrix.shape[0]
    panels = rows // orbitals
    spread = (lax.broadcasted_iota(jnp.int32, (rows, orbitals), 0) // panels == lax.broadcasted_iota(jnp.int32, (rows, orbitals), 1)).astype(F32)
    same = (lax.broadcasted_iota(jnp.int32, (rows, rows), 0) % panels == lax.broadcasted_iota(jnp.int32, (rows, rows), 1) % panels).astype(F32)
    return exact(exact(spread, matrix, ((1,), (0,))), spread, ((1,), (1,))) * same


def early_body(n_early, slot_of, groups, deal_ref, columns_ref, consts_ref, ham_ref, panel_ref, block_ref, other_ref, *refs):
    early = refs[:n_early]
    weights_ref, base_ref = refs[n_early:n_early + 2]
    sigmas = refs[n_early + 2:]
    orbitals = ham_ref.shape[0]
    lanes = 2 * orbitals
    rows = panel_ref.shape[1]
    mem, hist = lax.axis_index("mem"), lax.axis_index("hist")
    pair = mem >> 1
    slots, columns = block_ref.shape[0], block_ref.shape[1]

    consts = tuple(consts_ref[at] for at in range(4))
    for source, sigma in zip(early, sigmas):
        tiles = sigma_tiles(source[...].reshape((-1,) + source.shape[3:]), consts)
        sigma[...] = tiles.astype(BF16).reshape(source.shape)

    ham = row_matrix(ham_ref[...].astype(F32), rows).astype(BF16)
    sign = jnp.where(lax.broadcasted_iota(jnp.int32, (rows, lanes), 1) < orbitals, 1.0, -1.0).astype(F32)
    for tile in range(panel_ref.shape[0]):
        values = panel_ref[tile]
        turned = pltpu.roll(dot(ham, values), orbitals, 1) * sign
        base_ref[tile] = values.astype(F32) + time_step * turned

    flip = jnp.where(lax.broadcasted_iota(jnp.int32, (orbitals, lanes), 1) < orbitals, -1.0, 1.0).astype(F32)
    own_column = pair // groups
    for q in range(2 * slots):
        foreign, local = slot_of(q, hist)
        source = other_ref if foreign else block_ref
        mem_of = (mem ^ 1) if foreign else mem
        time = deal_ref[mem_of * slots + local]
        for apart in range(columns):
            column = own_column ^ apart
            keep = time >= columns_ref[hist * columns + column]
            upper = source[local, column].astype(F32) * jnp.where(keep, 1.0, 0.0).astype(F32)
            lower = pltpu.roll(upper, orbitals, 1) * flip
            weights_ref[q * lanes:q * lanes + orbitals, apart * lanes:(apart + 1) * lanes] = upper.astype(BF16)
            weights_ref[q * lanes + orbitals:(q + 1) * lanes, apart * lanes:(apart + 1) * lanes] = lower.astype(BF16)


def term_body(n_done, n_late, places, groups, consts_ref, weights_ref, *refs):
    done, late = refs[:n_done], refs[n_done:n_done + n_late]
    outs, left_ref = refs[n_done + n_late:-1], refs[-1]
    pair = lax.axis_index("mem") >> 1
    own_group = pair % groups
    consts = tuple(consts_ref[at] for at in range(4))
    rows, lanes = outs[0].shape[1:]
    for step in range(groups):
        group = own_group ^ step
        q = 0
        for at, source in enumerate(done + late):
            tiles = source[:, group]
            count = tiles.shape[0]
            if at >= n_done:
                tiles = sigma_tiles(tiles.reshape((-1,) + tiles.shape[2:]), consts).astype(BF16).reshape(tiles.shape)
            for s in range(count):
                left_ref[:, q * lanes:(q + 1) * lanes] = tiles[s].reshape(rows, lanes)
                q += 1
        total = dot(left_ref[...], weights_ref[...])
        for block, (to, place) in places.items():
            if block % groups == step:
                apart = block // groups
                value = total[:, apart * lanes:(apart + 1) * lanes]
                outs[to][place] = value.astype(outs[to].dtype)


def add_body(n_got, keep_ref, *refs):
    gots, outs = refs[:n_got], refs[n_got:]
    total = keep_ref[...]
    for got in gots:
        total = total + got[...].astype(F32)
    size = outs[0].shape[0]
    for at, out in enumerate(outs):
        out[...] = total[at * size:(at + 1) * size].astype(out.dtype)


def last_body(counts, consts_ref, base_ref, *refs):
    chunks = len(counts)
    keeps, gots = refs[:chunks], refs[chunks:-2]
    rows_ref, sigma_ref = refs[-2:]
    consts = tuple(consts_ref[at] for at in range(4))
    size = base_ref.shape[0] // chunks
    for c in range(chunks):
        here = slice(c * size, (c + 1) * size)
        collision = keeps[c][...]
        for got in gots[:counts[c]]:
            collision = collision + got[...].astype(F32)
        gots = gots[counts[c]:]
        collision = collision.reshape((size,) + base_ref.shape[1:])
        rows = (base_ref[here] + time_step * collision).astype(BF16)
        rows_ref[here] = rows
        sigma_ref[here] = sigma_tiles(rows, consts).astype(BF16)


def step_masks(count):
    bits = [1 << b for b in range(count.bit_length() - 1)]
    steps = []
    while bits:
        take = 1 if len(bits) % 2 else 2
        here, bits = bits[:take], bits[take:]
        masks = [0]
        for bit in here:
            masks = masks + [mask ^ bit for mask in masks]
        steps.append(masks[2:] + masks[1:2] + [0] if take == 2 else masks[::-1])
    return steps


def block_places(steps, parts):
    def spread(rest):
        if not rest:
            return [0]
        inner = spread(rest[1:])
        return [mask ^ block for mask in rest[0] for block in inner]

    inner = spread(steps[1:])
    size = len(inner) // parts
    return {mask ^ block: (place // size * len(steps[0]) + to, place % size) for to, mask in enumerate(steps[0]) for place, block in enumerate(inner)}


def exchange(value, mem_mask, hist_mask):
    mems, hists = lax.axis_size("mem"), lax.axis_size("hist")
    pairs = [(m * hists + h, (m ^ mem_mask) * hists + (h ^ hist_mask)) for m in range(mems) for h in range(hists)]
    return lax.ppermute(value, ("mem", "hist"), pairs)


def local(memory_block, memory_rows, panel_rows, time_deal, column_times, window_start, coupling, hamiltonian):
    orbitals = coupling.shape[0]
    panels, lanes = panel_rows.shape[1:]
    rows = orbitals * panels
    slots = memory_block.shape[0]
    columns = memory_block.shape[1]
    pairs = lax.axis_size("mem") // 2
    own_tiles = panel_rows.shape[0] // orbitals
    groups = P_SIZE // (2 * own_tiles)
    chunks = CHUNKS if own_tiles % CHUNKS == 0 else 1
    part = own_tiles // chunks
    two_hist = lax.axis_size("hist") == 2

    if not two_hist:
        memory_rows = lax.all_gather(memory_rows, "hist", axis=0, tiled=True)
    held = memory_rows.shape[0] // (P_SIZE * orbitals)
    tiles = memory_rows.reshape(held, groups, 2, own_tiles, rows, lanes)
    panel_tiles = panel_rows.reshape(own_tiles, rows, lanes)
    piece = shape((held, groups, part, rows, lanes), BF16)
    smem = pl.BlockSpec(memory_space=pltpu.SMEM)
    vmem = pl.BlockSpec(memory_space=pltpu.VMEM)
    split = call(split_body, [piece] * (2 * chunks), tiles, in_specs=[vmem], flops=PREFETCH_FLOPS)
    mine, other = list(split[0::2]), list(split[1::2])

    kept_times = jnp.where(time_deal >= window_start, time_deal, jnp.iinfo(jnp.int32).min)
    ready_in = [array for c in range(1, chunks) for array in (mine[c], other[c])]
    consts, *ready = call(
        functools.partial(ready_body, len(ready_in)),
        [shape((4, rows, lanes), BF16)] + [piece] * len(ready_in),
        coupling, *ready_in,
        in_specs=[vmem] * (1 + len(ready_in)),
    )
    mine[1:], other[1:] = ready[0::2], ready[1::2]
    partner_block = exchange(memory_block, 1, 0)
    partner = [exchange(other[c], 1, 0) for c in range(chunks)]
    if two_hist:
        same_core = [exchange(mine[c], 0, 1) for c in range(chunks)]
        cross = [exchange(other[c], 1, 1) for c in range(chunks)]

    if two_hist:
        def slot_of(q, hist):
            return (q // held) % 2, (hist ^ (q // (2 * held))) * held + q % held
    else:
        def slot_of(q, hist):
            return q // held, q % held

    outs = [shape((2 * slots * lanes, columns * lanes), BF16), shape((own_tiles, rows, lanes), F32), piece, piece]
    weights, base, *sigmas = call(
        functools.partial(early_body, 2, slot_of, groups),
        outs,
        kept_times, column_times, consts, hamiltonian, panel_tiles, memory_block, partner_block, mine[0], partner[0],
        in_specs=[smem] * 2 + [vmem] * 7,
    )

    keeps, received = [], []
    for c in range(chunks):
        steps = step_masks(pairs)
        if c < chunks - 1:
            steps = steps[1:] + steps[:1]
        parts = 2 if c == chunks - 1 and len(steps) > 1 else 1
        height = part * rows
        done = list(sigmas) if c == 0 else [mine[c], partner[c]]
        late = []
        if two_hist:
            if c == 0:
                late = [same_core[c], cross[c]]
            else:
                done += [same_core[c], cross[c]]
        count = pairs // len(steps[0]) // parts

        def pieces(masks, count):
            return [shape((count, height, lanes), BF16 if mask else F32) for mask in masks]

        outs = call(
            functools.partial(term_body, len(done), len(late), block_places(steps, parts), groups),
            pieces(steps[0], count) * parts,
            consts, weights, *done, *late,
            flops=2 * height * groups * 2 * slots * lanes * columns * lanes,
            scratch_shapes=[pltpu.VMEM((height, 2 * slots * lanes), BF16)],
        )
        size = len(steps[0])
        state = [(outs[p * size:(p + 1) * size - 1], outs[(p + 1) * size - 1]) for p in range(parts)]
        for at, masks in enumerate(steps):
            gots = [[exchange(sends[i], 2 * masks[i], 0) for i in range(len(sends))] for sends, _ in state]
            if at + 1 == len(steps):
                break
            after = steps[at + 1]
            share = len(after) // len(state)
            count = count * len(state) // len(after)
            outs = []
            for p, (_, keep) in enumerate(state):
                outs += call(functools.partial(add_body, len(gots[p])), pieces(after[p * share:(p + 1) * share], count), keep, *gots[p])
            state = [(outs[:-1], outs[-1])]
        keeps.append(state[0][1])
        received.append(gots[0])

    result = shape((own_tiles, rows, lanes), BF16)
    new_rows, new_sigma = call(
        functools.partial(last_body, [len(gots) for gots in received]),
        [result, result],
        consts, base, *keeps, *[got for gots in received for got in gots],
    )
    return new_rows.reshape(panel_rows.shape), new_sigma.reshape(panel_rows.shape)


def solution(mesh):
    in_specs = (
        P("mem", "hist", None, None),
        P(("mem", "hist"), None, None),
        P(("hist", "mem"), None, None),
        P(),
        P(),
        P(),
        P(),
        P(),
    )
    out_specs = (P(("hist", "mem"), None, None), P(("hist", "mem"), None, None))
    return jax.shard_map(local, mesh=mesh, in_specs=in_specs, out_specs=out_specs, check_vma=False)
```

```python
import functools

import jax
import jax.numpy as jnp
from jax import lax
from jax.experimental import pallas as pl
from jax.experimental.pallas import tpu as pltpu
from jax.sharding import PartitionSpec as P


P_SIZE = 8
CHUNKS = 2
PREFETCH_FLOPS = 2_000_000_000


time_step = 0.02
F32 = jnp.float32
BF16 = jnp.bfloat16


def dot(left, right):
    return jnp.dot(left, right, preferred_element_type=F32)


def halves(value):
    top = value.astype(BF16)
    return top, (value - top.astype(F32)).astype(BF16)


def sigma_tiles(tiles, consts):
    n, rows, lanes = tiles.shape
    right_top, right_low, left_top, left_low = consts
    flat = tiles.reshape(n * rows, lanes).astype(F32)
    top, low = halves(flat * flat)
    screened = dot(top, right_top) + (dot(low, right_top) + dot(top, right_low))
    top, low = halves(screened)
    top, low = top.reshape(n, rows, lanes), low.reshape(n, rows, lanes)
    out = []
    step = 2 if n % 2 == 0 else 1
    for start in range(0, n, step):
        tops = jnp.concatenate([top[start + s] for s in range(step)], 1)
        lows = jnp.concatenate([low[start + s] for s in range(step)], 1)
        both = dot(left_top, tops) + (dot(left_top, lows) + dot(left_low, tops))
        for s in range(step):
            out.append(both[:, s * lanes:(s + 1) * lanes])
    screening = jnp.stack(out).reshape(n * rows, lanes)
    return (-flat * screening).reshape(n, rows, lanes)


def call(body, outs, *args, flops=0, grant=16, **keywords):
    moved = sum(a.size * a.dtype.itemsize for a in jax.tree.leaves((args, outs)))
    return pl.pallas_call(
        body,
        out_shape=outs,
        cost_estimate=pl.CostEstimate(flops=flops, bytes_accessed=moved, transcendentals=0),
        compiler_params=pltpu.CompilerParams(vmem_limit_bytes=grant << 20),
        **keywords,
    )(*args)


def shape(dims, kind):
    return jax.ShapeDtypeStruct(tuple(dims), kind)


def split_body(rows_ref, *outs):
    core = lax.axis_index("mem") & 1
    for at, out in enumerate(outs):
        size = out.shape[2]
        first = (at // 2) * size
        out[...] = rows_ref[:, :, core if at % 2 == 0 else 1 - core, first:first + size]


def ready_body(count, coupling_ref, *refs):
    sources, consts_ref, sigmas = refs[:count], refs[count], refs[count + 1:]
    rows, lanes = consts_ref.shape[1:]
    orbitals = lanes // 2
    fold = one_hot(lanes, orbitals, lambda at: at % orbitals)
    consts = []
    for part in halves(coupling_ref[...]):
        consts.append(across(across(fold, part).astype(BF16), fold).astype(BF16))
    consts = [*consts, *(row_matrix(part, rows) for part in halves(coupling_ref[...]))]
    for at, value in enumerate(consts):
        consts_ref[at] = value
    for source, sigma in zip(sources, sigmas):
        tiles = sigma_tiles(source[...].reshape((-1,) + source.shape[3:]), consts)
        sigma[...] = tiles.astype(BF16).reshape(source.shape)


def one_hot(rows, orbitals, orbital_of):
    at = lax.broadcasted_iota(jnp.int32, (rows, orbitals), 0)
    return (orbital_of(at) == lax.broadcasted_iota(jnp.int32, (rows, orbitals), 1)).astype(F32).astype(BF16)


def across(left, right):
    return lax.dot_general(left, right, (((1,), (1,)), ((), ())), preferred_element_type=F32)


def row_matrix(matrix, rows):
    orbitals = matrix.shape[0]
    panels = rows // orbitals
    spread = one_hot(rows, orbitals, lambda at: at // panels)
    row_at = lax.broadcasted_iota(jnp.int32, (rows, rows), 0)
    lane_at = lax.broadcasted_iota(jnp.int32, (rows, rows), 1)
    spreaded = across(dot(spread, matrix).astype(BF16), spread)
    return jnp.where(row_at % panels == lane_at % panels, spreaded, 0.0).astype(BF16)


def early_body(n_early, slot_of, groups, deal_ref, columns_ref, consts_ref, block_ref, other_ref, *refs):
    early = refs[:n_early]
    weights_ref, sigmas = refs[n_early], refs[n_early + 1:]
    orbitals, lanes = block_ref.shape[2:]
    mem, hist = lax.axis_index("mem"), lax.axis_index("hist")
    pair = mem >> 1
    slots, columns = block_ref.shape[0], block_ref.shape[1]

    consts = tuple(consts_ref[at] for at in range(4))
    for source, sigma in zip(early, sigmas):
        tiles = sigma_tiles(source[...].reshape((-1,) + source.shape[3:]), consts)
        sigma[...] = tiles.astype(BF16).reshape(source.shape)

    flip = jnp.where(lax.broadcasted_iota(jnp.int32, (orbitals, lanes), 1) < orbitals, -1.0, 1.0).astype(F32)
    own_column = pair // groups
    for q in range(2 * slots):
        foreign, local = slot_of(q, hist)
        source = other_ref if foreign else block_ref
        mem_of = (mem ^ 1) if foreign else mem
        time = deal_ref[mem_of * slots + local]
        for apart in range(columns):
            column = own_column ^ apart
            keep = time >= columns_ref[hist * columns + column]
            upper = source[local, column].astype(F32) * jnp.where(keep, 1.0, 0.0).astype(F32)
            lower = pltpu.roll(upper, orbitals, 1) * flip
            weights_ref[q * lanes:q * lanes + orbitals, apart * lanes:(apart + 1) * lanes] = upper.astype(BF16)
            weights_ref[q * lanes + orbitals:(q + 1) * lanes, apart * lanes:(apart + 1) * lanes] = lower.astype(BF16)


def term_body(n_done, n_late, places, groups, consts_ref, weights_ref, *refs):
    done, late = refs[:n_done], refs[n_done:n_done + n_late]
    outs, left_ref = refs[n_done + n_late:-1], refs[-1]
    pair = lax.axis_index("mem") >> 1
    own_group = pair % groups
    consts = tuple(consts_ref[at] for at in range(4))
    rows, lanes = outs[0].shape[1:]
    for step in range(groups):
        group = own_group ^ step
        q = 0
        for at, source in enumerate(done + late):
            tiles = source[:, group]
            count = tiles.shape[0]
            if at >= n_done:
                tiles = sigma_tiles(tiles.reshape((-1,) + tiles.shape[2:]), consts).astype(BF16).reshape(tiles.shape)
            for s in range(count):
                left_ref[:, q * lanes:(q + 1) * lanes] = tiles[s].reshape(rows, lanes)
                q += 1
        total = dot(left_ref[...], weights_ref[...])
        for block, (to, place) in places.items():
            if block % groups == step:
                apart = block // groups
                value = total[:, apart * lanes:(apart + 1) * lanes]
                outs[to][place] = value.astype(outs[to].dtype)


def add_body(n_got, keep_ref, *refs):
    gots, outs = refs[:n_got], refs[n_got:]
    total = keep_ref[...]
    for got in gots:
        total = total + got[...].astype(F32)
    size = outs[0].shape[0]
    for at, out in enumerate(outs):
        out[...] = total[at * size:(at + 1) * size].astype(out.dtype)


def base_body(ham_ref, panel_ref, base_ref):
    rows, lanes = panel_ref.shape[1:]
    orbitals = ham_ref.shape[0]
    ham = row_matrix(ham_ref[...], rows)
    sign = jnp.where(lax.broadcasted_iota(jnp.int32, (rows, lanes), 1) < orbitals, 1.0, -1.0).astype(F32)
    for tile in range(panel_ref.shape[0]):
        values = panel_ref[tile]
        turned = pltpu.roll(dot(ham, values), orbitals, 1) * sign
        base_ref[tile] = values.astype(F32) + time_step * turned


def last_body(c, n_got, consts_ref, base_ref, keep_ref, *refs):
    gots = refs[:n_got]
    rows_out, sigma_out, rows_ref, sigma_ref, sems = refs[-5:]
    size = rows_ref.shape[0]
    here = pl.ds(c * size, size)
    collision = keep_ref[...]
    for got in gots:
        collision = collision + got[...].astype(F32)
    collision = collision.reshape(rows_ref.shape)
    rows_ref[...] = (base_ref[here] + time_step * collision).astype(BF16)
    rows_copy = pltpu.make_async_copy(rows_ref, rows_out.at[here], sems.at[0])
    rows_copy.start()
    sigma_ref[...] = sigma_tiles(rows_ref[...], tuple(consts_ref[at] for at in range(4))).astype(BF16)
    sigma_copy = pltpu.make_async_copy(sigma_ref, sigma_out.at[here], sems.at[1])
    sigma_copy.start()
    rows_copy.wait()
    sigma_copy.wait()


def step_masks(count):
    bits = [1 << b for b in range(count.bit_length() - 1)]
    steps = []
    while bits:
        take = 1 if len(bits) % 2 else 2
        here, bits = bits[:take], bits[take:]
        masks = [0]
        for bit in here:
            masks = masks + [mask ^ bit for mask in masks]
        steps.append(masks[2:] + masks[1:2] + [0] if take == 2 else masks[::-1])
    return steps


def block_places(steps, parts):
    def spread(rest):
        if not rest:
            return [0]
        inner = spread(rest[1:])
        return [mask ^ block for mask in rest[0] for block in inner]

    inner = spread(steps[1:])
    size = len(inner) // parts
    return {mask ^ block: (place // size * len(steps[0]) + to, place % size) for to, mask in enumerate(steps[0]) for place, block in enumerate(inner)}


def exchange(value, mem_mask, hist_mask):
    mems, hists = lax.axis_size("mem"), lax.axis_size("hist")
    pairs = [(m * hists + h, (m ^ mem_mask) * hists + (h ^ hist_mask)) for m in range(mems) for h in range(hists)]
    return lax.ppermute(value, ("mem", "hist"), pairs)


def local(memory_block, memory_rows, panel_rows, time_deal, column_times, window_start, coupling, hamiltonian):
    orbitals = coupling.shape[0]
    panels, lanes = panel_rows.shape[1:]
    rows = orbitals * panels
    slots = memory_block.shape[0]
    columns = memory_block.shape[1]
    pairs = lax.axis_size("mem") // 2
    own_tiles = panel_rows.shape[0] // orbitals
    groups = P_SIZE // (2 * own_tiles)
    chunks = CHUNKS if own_tiles % CHUNKS == 0 else 1
    part = own_tiles // chunks
    two_hist = lax.axis_size("hist") == 2

    if not two_hist:
        memory_rows = lax.all_gather(memory_rows, "hist", axis=0, tiled=True)
    held = memory_rows.shape[0] // (P_SIZE * orbitals)
    tiles = memory_rows.reshape(held, groups, 2, own_tiles, rows, lanes)
    panel_tiles = panel_rows.reshape(own_tiles, rows, lanes)
    piece = shape((held, groups, part, rows, lanes), BF16)
    smem = pl.BlockSpec(memory_space=pltpu.SMEM)
    vmem = pl.BlockSpec(memory_space=pltpu.VMEM)
    split = call(split_body, [piece] * (2 * chunks), tiles, in_specs=[vmem], flops=PREFETCH_FLOPS)
    mine, other = list(split[0::2]), list(split[1::2])

    kept_times = jnp.where(time_deal >= window_start, time_deal, jnp.iinfo(jnp.int32).min)
    ready_in = [array for c in range(1, chunks) for array in (mine[c], other[c])]
    consts, *ready = call(
        functools.partial(ready_body, len(ready_in)),
        [shape((4, rows, lanes), BF16)] + [piece] * len(ready_in),
        coupling, *ready_in,
        in_specs=[vmem] * (1 + len(ready_in)),
    )
    mine[1:], other[1:] = ready[0::2], ready[1::2]
    partner_block = exchange(memory_block, 1, 0)
    partner = [exchange(other[c], 1, 0) for c in range(chunks)]
    if two_hist:
        same_core = [exchange(mine[c], 0, 1) for c in range(chunks)]
        cross = [exchange(other[c], 1, 1) for c in range(chunks)]

    if two_hist:
        def slot_of(q, hist):
            return (q // held) % 2, (hist ^ (q // (2 * held))) * held + q % held
    else:
        def slot_of(q, hist):
            return q // held, q % held

    outs = [shape((2 * slots * lanes, columns * lanes), BF16), piece, piece]
    weights, *sigmas = call(
        functools.partial(early_body, 2, slot_of, groups),
        outs,
        kept_times, column_times, consts, memory_block, partner_block, mine[0], partner[0],
        in_specs=[smem] * 2 + [vmem] * 5,
    )

    keeps, received = [], []
    for c in range(chunks):
        steps = step_masks(pairs)
        if c < chunks - 1:
            steps = steps[1:] + steps[:1]
        parts = 2 if c == chunks - 1 and len(steps) > 1 else 1
        height = part * rows
        done = list(sigmas) if c == 0 else [mine[c], partner[c]]
        late = []
        if two_hist:
            if c == 0:
                late = [same_core[c], cross[c]]
            else:
                done += [same_core[c], cross[c]]
        count = pairs // len(steps[0]) // parts

        def pieces(masks, count):
            return [shape((count, height, lanes), BF16 if mask else F32) for mask in masks]

        def term(places, outs):
            return call(
                functools.partial(term_body, len(done), len(late), places, groups),
                outs,
                consts, weights, *done, *late,
                flops=2 * height * groups * 2 * slots * lanes * columns * lanes,
                scratch_shapes=[pltpu.VMEM((height, 2 * slots * lanes), BF16)],
            )

        if c < chunks - 1 and len(steps) == 2 and len(steps[0]) == 4:
            (near, far, side, _), (last, _) = steps
            places = {near ^ last: (0, 0), near: (0, 1), far ^ last: (1, 0), far: (2, 0), side ^ last: (3, 0), side: (3, 1), last: (4, 0), 0: (4, 1)}
            sizes = ((2, BF16), (1, BF16), (1, F32), (2, BF16), (2, F32))
            to_near, to_last, to_far, to_side, keep = term(places, [shape((count, height, lanes), kind) for count, kind in sizes])
            got_near = exchange(to_near, 2 * near, 0)
            (to_far,) = call(functools.partial(add_body, 1), [shape((1, height, lanes), BF16)], to_far, exchange(to_last, 2 * last, 0))
            got_far = exchange(to_far, 2 * far, 0)
            got_side = exchange(to_side, 2 * side, 0)
            send, keep = call(functools.partial(add_body, 2), [shape((1, height, lanes), kind) for kind in (BF16, F32)], keep, got_near, got_side)
            keeps.append(keep)
            received.append([exchange(send, 2 * last, 0), got_far])
            continue

        outs = term(block_places(steps, parts), pieces(steps[0], count) * parts)
        size = len(steps[0])
        state = [(outs[p * size:(p + 1) * size - 1], outs[(p + 1) * size - 1]) for p in range(parts)]
        for at, masks in enumerate(steps):
            gots = [[exchange(sends[i], 2 * masks[i], 0) for i in range(len(sends))] for sends, _ in state]
            if at + 1 == len(steps):
                break
            after = steps[at + 1]
            share = len(after) // len(state)
            count = count * len(state) // len(after)
            outs = []
            for p, (_, keep) in enumerate(state):
                outs += call(functools.partial(add_body, len(gots[p])), pieces(after[p * share:(p + 1) * share], count), keep, *gots[p])
            state = [(outs[:-1], outs[-1])]
        keeps.append(state[0][1])
        received.append(gots[0])

    base = call(base_body, shape((own_tiles, rows, lanes), F32), hamiltonian, panel_tiles)
    anywhere = pl.BlockSpec(memory_space=pl.ANY)
    result = []
    for c in range(chunks):
        given = [consts, base, keeps[c], *received[c]]
        result = call(
            functools.partial(last_body, c, len(received[c])),
            [shape((own_tiles, rows, lanes), BF16)] * 2,
            *given, *result,
            in_specs=[vmem] * len(given) + [anywhere] * len(result),
            out_specs=[anywhere] * 2,
            input_output_aliases={len(given) + at: at for at in range(len(result))},
            scratch_shapes=[pltpu.VMEM((part, rows, lanes), BF16)] * 2 + [pltpu.SemaphoreType.DMA((2,))],
        )
    new_rows, new_sigma = result
    return new_rows.reshape(panel_rows.shape), new_sigma.reshape(panel_rows.shape)


def solution(mesh):
    in_specs = (
        P("mem", "hist", None, None),
        P(("mem", "hist"), None, None),
        P(("hist", "mem"), None, None),
        P(),
        P(),
        P(),
        P(),
        P(),
    )
    out_specs = (P(("hist", "mem"), None, None), P(("hist", "mem"), None, None))
    return jax.shard_map(local, mesh=mesh, in_specs=in_specs, out_specs=out_specs, check_vma=False)
```

```python
import functools

import jax
import jax.numpy as jnp
from jax import lax
from jax.experimental import pallas as pl
from jax.experimental.pallas import tpu as pltpu
from jax.sharding import PartitionSpec as P


P_SIZE = 8
CHUNKS = 2
PREFETCH_FLOPS = 2_000_000_000


time_step = 0.02
CUTS = {2: (1,), 4: (2,)}
F32 = jnp.float32
BF16 = jnp.bfloat16


def dot(left, right):
    return jnp.dot(left, right, preferred_element_type=F32)


def halves(value):
    top = value.astype(BF16)
    return top, (value - top.astype(F32)).astype(BF16)


def sigma_tiles(tiles, consts):
    n, rows, lanes = tiles.shape
    right_top, right_low, left_top, left_low = consts
    flat = tiles.reshape(n * rows, lanes).astype(F32)
    top, low = halves(flat * flat)
    screened = dot(top, right_top) + (dot(low, right_top) + dot(top, right_low))
    top, low = halves(screened)
    top, low = top.reshape(n, rows, lanes), low.reshape(n, rows, lanes)
    out = []
    step = 2 if n % 2 == 0 else 1
    for start in range(0, n, step):
        tops = jnp.concatenate([top[start + s] for s in range(step)], 1)
        lows = jnp.concatenate([low[start + s] for s in range(step)], 1)
        both = dot(left_top, tops) + (dot(left_top, lows) + dot(left_low, tops))
        for s in range(step):
            out.append(both[:, s * lanes:(s + 1) * lanes])
    screening = jnp.stack(out).reshape(n * rows, lanes)
    return (-flat * screening).reshape(n, rows, lanes)


def call(body, outs, *args, flops=0, grant=16, **keywords):
    moved = sum(a.size * a.dtype.itemsize for a in jax.tree.leaves((args, outs)))
    return pl.pallas_call(
        body,
        out_shape=outs,
        cost_estimate=pl.CostEstimate(flops=flops, bytes_accessed=moved, transcendentals=0),
        compiler_params=pltpu.CompilerParams(vmem_limit_bytes=grant << 20),
        **keywords,
    )(*args)


def shape(dims, kind):
    return jax.ShapeDtypeStruct(tuple(dims), kind)


def split_body(rows_ref, *outs):
    core = lax.axis_index("mem") & 1
    for at, out in enumerate(outs):
        size = out.shape[2]
        first = (at // 2) * size
        out[...] = rows_ref[:, :, core if at % 2 == 0 else 1 - core, first:first + size]


def ready_body(count, coupling_ref, *refs):
    sources, consts_ref, sigmas = refs[:count], refs[count], refs[count + 1:]
    rows, lanes = consts_ref.shape[1:]
    orbitals = lanes // 2
    fold = one_hot(lanes, orbitals, lambda at: at % orbitals)
    consts = []
    for part in halves(coupling_ref[...]):
        consts.append(across(across(fold, part).astype(BF16), fold).astype(BF16))
    consts = [*consts, *(row_matrix(part, rows) for part in halves(coupling_ref[...]))]
    for at, value in enumerate(consts):
        consts_ref[at] = value
    for source, sigma in zip(sources, sigmas):
        tiles = sigma_tiles(source[...].reshape((-1,) + source.shape[3:]), consts)
        sigma[...] = tiles.astype(BF16).reshape(source.shape)


def one_hot(rows, orbitals, orbital_of):
    at = lax.broadcasted_iota(jnp.int32, (rows, orbitals), 0)
    return (orbital_of(at) == lax.broadcasted_iota(jnp.int32, (rows, orbitals), 1)).astype(F32).astype(BF16)


def across(left, right):
    return lax.dot_general(left, right, (((1,), (1,)), ((), ())), preferred_element_type=F32)


def row_matrix(matrix, rows):
    orbitals = matrix.shape[0]
    panels = rows // orbitals
    spread = one_hot(rows, orbitals, lambda at: at // panels)
    row_at = lax.broadcasted_iota(jnp.int32, (rows, rows), 0)
    lane_at = lax.broadcasted_iota(jnp.int32, (rows, rows), 1)
    spreaded = across(dot(spread, matrix).astype(BF16), spread)
    return jnp.where(row_at % panels == lane_at % panels, spreaded, 0.0).astype(BF16)


def early_body(n_early, slot_of, groups, deal_ref, columns_ref, consts_ref, block_ref, other_ref, *refs):
    early = refs[:n_early]
    weights_ref, sigmas = refs[n_early], refs[n_early + 1:]
    orbitals, lanes = block_ref.shape[2:]
    mem, hist = lax.axis_index("mem"), lax.axis_index("hist")
    pair = mem >> 1
    slots, columns = block_ref.shape[0], block_ref.shape[1]

    consts = tuple(consts_ref[at] for at in range(4))
    for source, sigma in zip(early, sigmas):
        tiles = sigma_tiles(source[...].reshape((-1,) + source.shape[3:]), consts)
        sigma[...] = tiles.astype(BF16).reshape(source.shape)

    flip = jnp.where(lax.broadcasted_iota(jnp.int32, (orbitals, lanes), 1) < orbitals, -1.0, 1.0).astype(F32)
    own_column = pair // groups
    for q in range(2 * slots):
        foreign, local = slot_of(q, hist)
        source = other_ref if foreign else block_ref
        mem_of = (mem ^ 1) if foreign else mem
        time = deal_ref[mem_of * slots + local]
        for apart in range(columns):
            column = own_column ^ apart
            keep = time >= columns_ref[hist * columns + column]
            upper = source[local, column].astype(F32) * jnp.where(keep, 1.0, 0.0).astype(F32)
            lower = pltpu.roll(upper, orbitals, 1) * flip
            weights_ref[q * lanes:q * lanes + orbitals, apart * lanes:(apart + 1) * lanes] = upper.astype(BF16)
            weights_ref[q * lanes + orbitals:(q + 1) * lanes, apart * lanes:(apart + 1) * lanes] = lower.astype(BF16)


def term_body(n_done, n_late, places, groups, consts_ref, weights_ref, *refs):
    done, late = refs[:n_done], refs[n_done:n_done + n_late]
    outs, left_ref = refs[n_done + n_late:-1], refs[-1]
    pair = lax.axis_index("mem") >> 1
    own_group = pair % groups
    consts = tuple(consts_ref[at] for at in range(4))
    rows, lanes = outs[0].shape[1:]
    for step in range(groups):
        group = own_group ^ step
        q = 0
        for at, source in enumerate(done + late):
            tiles = source[:, group]
            count = tiles.shape[0]
            if at >= n_done:
                tiles = sigma_tiles(tiles.reshape((-1,) + tiles.shape[2:]), consts).astype(BF16).reshape(tiles.shape)
            for s in range(count):
                left_ref[:, q * lanes:(q + 1) * lanes] = tiles[s].reshape(rows, lanes)
                q += 1
        total = dot(left_ref[...], weights_ref[...])
        for block, (to, place) in places.items():
            if block % groups == step:
                apart = block // groups
                value = total[:, apart * lanes:(apart + 1) * lanes]
                outs[to][place] = value.astype(outs[to].dtype)


def add_body(n_got, keep_ref, *refs):
    gots, outs = refs[:n_got], refs[n_got:]
    total = keep_ref[...]
    for got in gots:
        total = total + got[...].astype(F32)
    size = outs[0].shape[0]
    for at, out in enumerate(outs):
        out[...] = total[at * size:(at + 1) * size].astype(out.dtype)


def base_body(ham_ref, panel_ref, base_ref):
    rows, lanes = panel_ref.shape[1:]
    orbitals = ham_ref.shape[0]
    ham = row_matrix(ham_ref[...], rows)
    sign = jnp.where(lax.broadcasted_iota(jnp.int32, (rows, lanes), 1) < orbitals, 1.0, -1.0).astype(F32)
    for tile in range(panel_ref.shape[0]):
        values = panel_ref[tile]
        turned = pltpu.roll(dot(ham, values), orbitals, 1) * sign
        base_ref[tile] = values.astype(F32) + time_step * turned


def advanced(base, keep_ref, gots):
    collision = keep_ref[...]
    for got in gots:
        collision = collision + got[...].astype(F32)
    return (base + time_step * collision.reshape(base.shape)).astype(BF16)


def new_sigma_of(rows, consts_ref):
    return sigma_tiles(rows, tuple(consts_ref[at] for at in range(4))).astype(BF16)


def finish_body(c, consts_ref, base_ref, keep_ref, *refs):
    gots, (rows_ref, sigma_ref) = refs[:-2], refs[-2:]
    size = rows_ref.shape[0]
    rows = advanced(base_ref[c * size:(c + 1) * size], keep_ref, gots)
    rows_ref[...] = rows
    sigma_ref[...] = new_sigma_of(rows, consts_ref)


def last_body(n_done, consts_ref, base_ref, keep_ref, *refs):
    finished, gots = refs[:2 * n_done], refs[2 * n_done:-5]
    rows_out, sigma_out, rows_ref, sigma_ref, sems = refs[-5:]
    size = rows_ref.shape[0]

    def copy(source, at):
        return pltpu.make_async_copy(source, (rows_out, sigma_out)[at % 2].at[pl.ds(at // 2 * size, size)], sems.at[at])

    copies = [copy(source, at) for at, source in enumerate((*finished, rows_ref, sigma_ref))]
    for at in range(2 * n_done):
        copies[at].start()
    rows_ref[...] = advanced(base_ref[n_done * size:], keep_ref, gots)
    copies[-2].start()
    sigma_ref[...] = new_sigma_of(rows_ref[...], consts_ref)
    copies[-1].start()
    for started in copies:
        started.wait()


def step_masks(count):
    bits = [1 << b for b in range(count.bit_length() - 1)]
    steps = []
    while bits:
        take = 1 if len(bits) % 2 else 2
        here, bits = bits[:take], bits[take:]
        masks = [0]
        for bit in here:
            masks = masks + [mask ^ bit for mask in masks]
        steps.append(masks[2:] + masks[1:2] + [0] if take == 2 else masks[::-1])
    return steps


def block_places(steps, cuts):
    def spread(rest):
        if not rest:
            return [0]
        inner = spread(rest[1:])
        return [mask ^ block for mask in rest[0] for block in inner]

    inner = spread(steps[1:])
    places = {}
    for part, (start, stop) in enumerate(cuts):
        for to, mask in enumerate(steps[0]):
            for place in range(start, stop):
                places[mask ^ inner[place]] = (part * len(steps[0]) + to, place - start)
    return places


def exchange(value, mem_mask, hist_mask):
    mems, hists = lax.axis_size("mem"), lax.axis_size("hist")
    pairs = [(m * hists + h, (m ^ mem_mask) * hists + (h ^ hist_mask)) for m in range(mems) for h in range(hists)]
    return lax.ppermute(value, ("mem", "hist"), pairs)


def local(memory_block, memory_rows, panel_rows, time_deal, column_times, window_start, coupling, hamiltonian):
    orbitals = coupling.shape[0]
    panels, lanes = panel_rows.shape[1:]
    rows = orbitals * panels
    slots = memory_block.shape[0]
    columns = memory_block.shape[1]
    pairs = lax.axis_size("mem") // 2
    own_tiles = panel_rows.shape[0] // orbitals
    groups = P_SIZE // (2 * own_tiles)
    chunks = CHUNKS if own_tiles % CHUNKS == 0 else 1
    part = own_tiles // chunks
    two_hist = lax.axis_size("hist") == 2

    if not two_hist:
        memory_rows = lax.all_gather(memory_rows, "hist", axis=0, tiled=True)
    held = memory_rows.shape[0] // (P_SIZE * orbitals)
    tiles = memory_rows.reshape(held, groups, 2, own_tiles, rows, lanes)
    panel_tiles = panel_rows.reshape(own_tiles, rows, lanes)
    piece = shape((held, groups, part, rows, lanes), BF16)
    smem = pl.BlockSpec(memory_space=pltpu.SMEM)
    vmem = pl.BlockSpec(memory_space=pltpu.VMEM)
    split = call(split_body, [piece] * (2 * chunks), tiles, in_specs=[vmem], flops=PREFETCH_FLOPS)
    mine, other = list(split[0::2]), list(split[1::2])

    kept_times = jnp.where(time_deal >= window_start, time_deal, jnp.iinfo(jnp.int32).min)
    ready_in = [array for c in range(1, chunks) for array in (mine[c], other[c])]
    consts, *ready = call(
        functools.partial(ready_body, len(ready_in)),
        [shape((4, rows, lanes), BF16)] + [piece] * len(ready_in),
        coupling, *ready_in,
        in_specs=[vmem] * (1 + len(ready_in)),
    )
    mine[1:], other[1:] = ready[0::2], ready[1::2]
    partner_block = exchange(memory_block, 1, 0)
    partner = [exchange(other[c], 1, 0) for c in range(chunks)]
    if two_hist:
        same_core = [exchange(mine[c], 0, 1) for c in range(chunks)]
        cross = [exchange(other[c], 1, 1) for c in range(chunks)]

    if two_hist:
        def slot_of(q, hist):
            return (q // held) % 2, (hist ^ (q // (2 * held))) * held + q % held
    else:
        def slot_of(q, hist):
            return q // held, q % held

    outs = [shape((2 * slots * lanes, columns * lanes), BF16), piece, piece]
    weights, *sigmas = call(
        functools.partial(early_body, 2, slot_of, groups),
        outs,
        kept_times, column_times, consts, memory_block, partner_block, mine[0], partner[0],
        in_specs=[smem] * 2 + [vmem] * 5,
    )

    keeps, received = [], []
    for c in range(chunks):
        steps = step_masks(pairs)
        if c < chunks - 1:
            steps = steps[1:] + steps[:1]
        count = pairs // len(steps[0])
        cuts = [(0, count)]
        if c == chunks - 1 and len(steps) > 1:
            ends = [0, *CUTS[len(steps[1])], len(steps[1])]
            each = count // len(steps[1])
            cuts = [(start * each, stop * each) for start, stop in zip(ends, ends[1:])]
        height = part * rows
        done = list(sigmas) if c == 0 else [mine[c], partner[c]]
        late = []
        if two_hist:
            if c == 0:
                late = [same_core[c], cross[c]]
            else:
                done += [same_core[c], cross[c]]

        def pieces(masks, count):
            return [shape((count, height, lanes), BF16 if mask else F32) for mask in masks]

        def term(places, outs):
            return call(
                functools.partial(term_body, len(done), len(late), places, groups),
                outs,
                consts, weights, *done, *late,
                flops=2 * height * groups * 2 * slots * lanes * columns * lanes,
                scratch_shapes=[pltpu.VMEM((height, 2 * slots * lanes), BF16)],
            )

        if c < chunks - 1 and len(steps) == 2 and len(steps[0]) == 4:
            (near, far, side, _), (last, _) = steps
            places = {near ^ last: (0, 0), near: (0, 1), far ^ last: (1, 0), far: (2, 0), side ^ last: (3, 0), side: (3, 1), last: (4, 0), 0: (4, 1)}
            sizes = ((2, BF16), (1, BF16), (1, F32), (2, BF16), (2, F32))
            to_near, to_last, to_far, to_side, keep = term(places, [shape((count, height, lanes), kind) for count, kind in sizes])
            got_near = exchange(to_near, 2 * near, 0)
            (to_far,) = call(functools.partial(add_body, 1), [shape((1, height, lanes), BF16)], to_far, exchange(to_last, 2 * last, 0))
            got_far = exchange(to_far, 2 * far, 0)
            got_side = exchange(to_side, 2 * side, 0)
            send, keep = call(functools.partial(add_body, 2), [shape((1, height, lanes), kind) for kind in (BF16, F32)], keep, got_near, got_side)
            keeps.append(keep)
            received.append([exchange(send, 2 * last, 0), got_far])
            continue

        outs = term(block_places(steps, cuts), [piece for start, stop in cuts for piece in pieces(steps[0], stop - start)])
        size = len(steps[0])
        state = [(outs[p * size:(p + 1) * size - 1], outs[(p + 1) * size - 1]) for p in range(len(cuts))]
        for at, masks in enumerate(steps):
            gots = [[exchange(sends[i], 2 * masks[i], 0) for i in range(len(sends))] for sends, _ in state]
            if at + 1 == len(steps):
                break
            after = steps[at + 1]
            count //= len(after)
            outs = []
            for p, (_, keep) in enumerate(state):
                start, stop = (cut // count for cut in cuts[p])
                outs += call(functools.partial(add_body, len(gots[p])), pieces(after[start:stop], count), keep, *gots[p])
            cuts = [(0, count)]
            state = [(outs[:-1], outs[-1])]
        keeps.append(state[0][1])
        received.append(gots[0])

    base = call(base_body, shape((own_tiles, rows, lanes), F32), hamiltonian, panel_tiles)
    finished = []
    done_piece = [shape((part, rows, lanes), BF16)] * 2
    for c in range(chunks - 1):
        finished += call(functools.partial(finish_body, c), done_piece, consts, base, keeps[c], *received[c])
    given = [consts, base, keeps[-1], *finished, *received[-1]]
    new_rows, new_sigma = call(
        functools.partial(last_body, chunks - 1),
        [shape((own_tiles, rows, lanes), BF16)] * 2,
        *given,
        in_specs=[vmem] * len(given),
        out_specs=[pl.BlockSpec(memory_space=pl.ANY)] * 2,
        scratch_shapes=[pltpu.VMEM((part, rows, lanes), BF16)] * 2 + [pltpu.SemaphoreType.DMA((2 * chunks,))],
    )
    return new_rows.reshape(panel_rows.shape), new_sigma.reshape(panel_rows.shape)


def solution(mesh):
    in_specs = (
        P("mem", "hist", None, None),
        P(("mem", "hist"), None, None),
        P(("hist", "mem"), None, None),
        P(),
        P(),
        P(),
        P(),
        P(),
    )
    out_specs = (P(("hist", "mem"), None, None), P(("hist", "mem"), None, None))
    return jax.shard_map(local, mesh=mesh, in_specs=in_specs, out_specs=out_specs, check_vma=False)
```

```python
import functools

import jax
import jax.numpy as jnp
from jax import lax
from jax.experimental import pallas as pl
from jax.experimental.pallas import tpu as pltpu
from jax.sharding import PartitionSpec as P


P_SIZE = 8
CHUNKS = 2
PREFETCH_FLOPS = 2_000_000_000


time_step = 0.02
CUTS = {2: (1,), 4: (1, 2)}
F32 = jnp.float32
BF16 = jnp.bfloat16


def dot(left, right):
    return jnp.dot(left, right, preferred_element_type=F32)


def halves(value):
    top = value.astype(BF16)
    return top, (value - top.astype(F32)).astype(BF16)


def sigma_tiles(tiles, consts):
    n, rows, lanes = tiles.shape
    right_top, right_low, left_top, left_low = consts
    flat = tiles.reshape(n * rows, lanes).astype(F32)
    top, low = halves(flat * flat)
    screened = dot(top, right_top) + (dot(low, right_top) + dot(top, right_low))
    top, low = halves(screened)
    top, low = top.reshape(n, rows, lanes), low.reshape(n, rows, lanes)
    out = []
    step = 2 if n % 2 == 0 else 1
    for start in range(0, n, step):
        tops = jnp.concatenate([top[start + s] for s in range(step)], 1)
        lows = jnp.concatenate([low[start + s] for s in range(step)], 1)
        both = dot(left_top, tops) + (dot(left_top, lows) + dot(left_low, tops))
        for s in range(step):
            out.append(both[:, s * lanes:(s + 1) * lanes])
    screening = jnp.stack(out).reshape(n * rows, lanes)
    return (-flat * screening).reshape(n, rows, lanes)


def call(body, outs, *args, flops=0, grant=16, **keywords):
    moved = sum(a.size * a.dtype.itemsize for a in jax.tree.leaves((args, outs)))
    return pl.pallas_call(
        body,
        out_shape=outs,
        cost_estimate=pl.CostEstimate(flops=flops, bytes_accessed=moved, transcendentals=0),
        compiler_params=pltpu.CompilerParams(vmem_limit_bytes=grant << 20),
        **keywords,
    )(*args)


def shape(dims, kind):
    return jax.ShapeDtypeStruct(tuple(dims), kind)


def split_body(rows_ref, *outs):
    core = lax.axis_index("mem") & 1
    for at, out in enumerate(outs):
        size = out.shape[2]
        first = (at // 2) * size
        out[...] = rows_ref[:, :, core if at % 2 == 0 else 1 - core, first:first + size]


def ready_body(count, coupling_ref, *refs):
    sources, consts_ref, sigmas = refs[:count], refs[count], refs[count + 1:]
    rows, lanes = consts_ref.shape[1:]
    orbitals = lanes // 2
    fold = one_hot(lanes, orbitals, lambda at: at % orbitals)
    consts = []
    for part in halves(coupling_ref[...]):
        consts.append(across(across(fold, part).astype(BF16), fold).astype(BF16))
    consts = [*consts, *(row_matrix(part, rows) for part in halves(coupling_ref[...]))]
    for at, value in enumerate(consts):
        consts_ref[at] = value
    for source, sigma in zip(sources, sigmas):
        tiles = sigma_tiles(source[...].reshape((-1,) + source.shape[3:]), consts)
        sigma[...] = tiles.astype(BF16).reshape(source.shape)


def one_hot(rows, orbitals, orbital_of):
    at = lax.broadcasted_iota(jnp.int32, (rows, orbitals), 0)
    return (orbital_of(at) == lax.broadcasted_iota(jnp.int32, (rows, orbitals), 1)).astype(F32).astype(BF16)


def across(left, right):
    return lax.dot_general(left, right, (((1,), (1,)), ((), ())), preferred_element_type=F32)


def row_matrix(matrix, rows):
    orbitals = matrix.shape[0]
    panels = rows // orbitals
    spread = one_hot(rows, orbitals, lambda at: at // panels)
    row_at = lax.broadcasted_iota(jnp.int32, (rows, rows), 0)
    lane_at = lax.broadcasted_iota(jnp.int32, (rows, rows), 1)
    spreaded = across(dot(spread, matrix).astype(BF16), spread)
    return jnp.where(row_at % panels == lane_at % panels, spreaded, 0.0).astype(BF16)


def early_body(n_early, slot_of, groups, deal_ref, columns_ref, consts_ref, block_ref, other_ref, *refs):
    early = refs[:n_early]
    weights_ref, sigmas = refs[n_early], refs[n_early + 1:]
    orbitals, lanes = block_ref.shape[2:]
    mem, hist = lax.axis_index("mem"), lax.axis_index("hist")
    pair = mem >> 1
    slots, columns = block_ref.shape[0], block_ref.shape[1]

    consts = tuple(consts_ref[at] for at in range(4))
    for source, sigma in zip(early, sigmas):
        tiles = sigma_tiles(source[...].reshape((-1,) + source.shape[3:]), consts)
        sigma[...] = tiles.astype(BF16).reshape(source.shape)

    flip = jnp.where(lax.broadcasted_iota(jnp.int32, (orbitals, lanes), 1) < orbitals, -1.0, 1.0).astype(F32)
    own_column = pair // groups
    for q in range(2 * slots):
        foreign, local = slot_of(q, hist)
        source = other_ref if foreign else block_ref
        mem_of = (mem ^ 1) if foreign else mem
        time = deal_ref[mem_of * slots + local]
        for apart in range(columns):
            column = own_column ^ apart
            keep = time >= columns_ref[hist * columns + column]
            upper = source[local, column].astype(F32) * jnp.where(keep, 1.0, 0.0).astype(F32)
            lower = pltpu.roll(upper, orbitals, 1) * flip
            weights_ref[q * lanes:q * lanes + orbitals, apart * lanes:(apart + 1) * lanes] = upper.astype(BF16)
            weights_ref[q * lanes + orbitals:(q + 1) * lanes, apart * lanes:(apart + 1) * lanes] = lower.astype(BF16)


def term_body(n_done, n_late, places, groups, skipped, consts_ref, weights_ref, *refs):
    begun, refs = refs[:bool(skipped)], refs[bool(skipped):]
    done, late = refs[:n_done], refs[n_done:n_done + n_late]
    outs, left_ref = refs[n_done + n_late:-1], refs[-1]
    pair = lax.axis_index("mem") >> 1
    own_group = pair % groups
    consts = tuple(consts_ref[at] for at in range(4))
    rows, lanes = outs[0].shape[1:]
    for step in range(groups):
        group = own_group ^ step
        q = 0
        for at, source in enumerate(done + late):
            tiles = source[:, group]
            count = tiles.shape[0]
            if at >= n_done:
                tiles = sigma_tiles(tiles.reshape((-1,) + tiles.shape[2:]), consts).astype(BF16).reshape(tiles.shape)
            for s in range(count):
                left_ref[:, q * lanes:(q + 1) * lanes] = tiles[s].reshape(rows, lanes)
                q += 1
        total = dot(left_ref[...], weights_ref[skipped * lanes:])
        if begun:
            total = begun[0][...] + total
        for block, (to, place) in places.items():
            if block % groups == step:
                apart = block // groups
                value = total[:, apart * lanes:(apart + 1) * lanes]
                outs[to][place] = value.astype(outs[to].dtype)


def begin_body(weights_ref, *refs):
    sources, begun_ref, left_ref = refs[:-2], refs[-2], refs[-1]
    rows, lanes = begun_ref.shape[0], sources[0].shape[-1]
    q = 0
    for source in sources:
        for s in range(source.shape[0]):
            left_ref[:, q * lanes:(q + 1) * lanes] = source[s, 0].reshape(rows, lanes)
            q += 1
    begun_ref[...] = dot(left_ref[...], weights_ref[:q * lanes])


def add_body(n_got, keep_ref, *refs):
    gots, outs = refs[:n_got], refs[n_got:]
    total = keep_ref[...]
    for got in gots:
        total = total + got[...].astype(F32)
    size = outs[0].shape[0]
    for at, out in enumerate(outs):
        out[...] = total[at * size:(at + 1) * size].astype(out.dtype)


def base_body(ham_ref, panel_ref, base_ref):
    rows, lanes = panel_ref.shape[1:]
    orbitals = ham_ref.shape[0]
    ham = row_matrix(ham_ref[...], rows)
    sign = jnp.where(lax.broadcasted_iota(jnp.int32, (rows, lanes), 1) < orbitals, 1.0, -1.0).astype(F32)
    for tile in range(panel_ref.shape[0]):
        values = panel_ref[tile]
        turned = pltpu.roll(dot(ham, values), orbitals, 1) * sign
        base_ref[tile] = values.astype(F32) + time_step * turned


def advanced(base, keep_ref, gots):
    collision = keep_ref[...]
    for got in gots:
        collision = collision + got[...].astype(F32)
    return (base + time_step * collision.reshape(base.shape)).astype(BF16)


def new_sigma_of(rows, consts_ref):
    return sigma_tiles(rows, tuple(consts_ref[at] for at in range(4))).astype(BF16)


def finish_body(c, consts_ref, base_ref, keep_ref, *refs):
    gots, (rows_ref, sigma_ref) = refs[:-2], refs[-2:]
    size = rows_ref.shape[0]
    rows = advanced(base_ref[c * size:(c + 1) * size], keep_ref, gots)
    rows_ref[...] = rows
    sigma_ref[...] = new_sigma_of(rows, consts_ref)


def last_body(n_done, consts_ref, base_ref, keep_ref, *refs):
    finished, gots = refs[:2 * n_done], refs[2 * n_done:-5]
    rows_out, sigma_out, rows_ref, sigma_ref, sems = refs[-5:]
    size = rows_ref.shape[0]

    def copy(source, at):
        return pltpu.make_async_copy(source, (rows_out, sigma_out)[at % 2].at[pl.ds(at // 2 * size, size)], sems.at[at])

    copies = [copy(source, at) for at, source in enumerate((*finished, rows_ref, sigma_ref))]
    for at in range(2 * n_done):
        copies[at].start()
    rows_ref[...] = advanced(base_ref[n_done * size:], keep_ref, gots)
    copies[-2].start()
    sigma_ref[...] = new_sigma_of(rows_ref[...], consts_ref)
    copies[-1].start()
    for started in copies:
        started.wait()


def step_masks(count):
    bits = [1 << b for b in range(count.bit_length() - 1)]
    steps = []
    while bits:
        take = 1 if len(bits) % 2 else 2
        here, bits = bits[:take], bits[take:]
        masks = [0]
        for bit in here:
            masks = masks + [mask ^ bit for mask in masks]
        steps.append(masks[2:] + masks[1:2] + [0] if take == 2 else masks[::-1])
    return steps


def block_places(steps, cuts):
    def spread(rest):
        if not rest:
            return [0]
        inner = spread(rest[1:])
        return [mask ^ block for mask in rest[0] for block in inner]

    inner = spread(steps[1:])
    places = {}
    for part, (start, stop) in enumerate(cuts):
        for to, mask in enumerate(steps[0]):
            for place in range(start, stop):
                places[mask ^ inner[place]] = (part * len(steps[0]) + to, place - start)
    return places


def exchange(value, mem_mask, hist_mask):
    mems, hists = lax.axis_size("mem"), lax.axis_size("hist")
    pairs = [(m * hists + h, (m ^ mem_mask) * hists + (h ^ hist_mask)) for m in range(mems) for h in range(hists)]
    return lax.ppermute(value, ("mem", "hist"), pairs)


def local(memory_block, memory_rows, panel_rows, time_deal, column_times, window_start, coupling, hamiltonian):
    orbitals = coupling.shape[0]
    panels, lanes = panel_rows.shape[1:]
    rows = orbitals * panels
    slots = memory_block.shape[0]
    columns = memory_block.shape[1]
    pairs = lax.axis_size("mem") // 2
    own_tiles = panel_rows.shape[0] // orbitals
    groups = P_SIZE // (2 * own_tiles)
    chunks = CHUNKS if own_tiles % CHUNKS == 0 else 1
    part = own_tiles // chunks
    two_hist = lax.axis_size("hist") == 2

    if not two_hist:
        memory_rows = lax.all_gather(memory_rows, "hist", axis=0, tiled=True)
    held = memory_rows.shape[0] // (P_SIZE * orbitals)
    tiles = memory_rows.reshape(held, groups, 2, own_tiles, rows, lanes)
    panel_tiles = panel_rows.reshape(own_tiles, rows, lanes)
    piece = shape((held, groups, part, rows, lanes), BF16)
    smem = pl.BlockSpec(memory_space=pltpu.SMEM)
    vmem = pl.BlockSpec(memory_space=pltpu.VMEM)
    split = call(split_body, [piece] * (2 * chunks), tiles, in_specs=[vmem], flops=PREFETCH_FLOPS)
    mine, other = list(split[0::2]), list(split[1::2])

    kept_times = jnp.where(time_deal >= window_start, time_deal, jnp.iinfo(jnp.int32).min)
    ready_in = [array for c in range(1, chunks) for array in (mine[c], other[c])]
    consts, *ready = call(
        functools.partial(ready_body, len(ready_in)),
        [shape((4, rows, lanes), BF16)] + [piece] * len(ready_in),
        coupling, *ready_in,
        in_specs=[vmem] * (1 + len(ready_in)),
    )
    mine[1:], other[1:] = ready[0::2], ready[1::2]
    partner_block = exchange(memory_block, 1, 0)
    partner = [exchange(other[c], 1, 0) for c in range(chunks)]
    if two_hist:
        same_core = [exchange(mine[c], 0, 1) for c in range(chunks)]
        cross = [exchange(other[c], 1, 1) for c in range(chunks)]

    if two_hist:
        def slot_of(q, hist):
            return (q // held) % 2, (hist ^ (q // (2 * held))) * held + q % held
    else:
        def slot_of(q, hist):
            return q // held, q % held

    outs = [shape((2 * slots * lanes, columns * lanes), BF16), piece, piece]
    weights, *sigmas = call(
        functools.partial(early_body, 2, slot_of, groups),
        outs,
        kept_times, column_times, consts, memory_block, partner_block, mine[0], partner[0],
        in_specs=[smem] * 2 + [vmem] * 5,
    )

    keeps, received = [], []
    for c in range(chunks):
        steps = step_masks(pairs)
        if c < chunks - 1:
            steps = steps[1:] + steps[:1]
        count = pairs // len(steps[0])
        cuts = [(0, count)]
        if c == chunks - 1 and len(steps) > 1:
            ends = [0, *CUTS[len(steps[1])], len(steps[1])]
            each = count // len(steps[1])
            cuts = [(start * each, stop * each) for start, stop in zip(ends, ends[1:])]
        height = part * rows
        done = list(sigmas) if c == 0 else [mine[c], partner[c]]
        late, begun, skipped = [], [], 0
        if two_hist:
            if c == 0:
                late = [same_core[c], cross[c]]
            elif groups == 1:
                skipped = sum(source.shape[0] for source in done)
                begun = [call(
                    begin_body,
                    shape((height, columns * lanes), F32),
                    weights, *done,
                    scratch_shapes=[pltpu.VMEM((height, skipped * lanes), BF16)],
                )]
                done = [same_core[c], cross[c]]
            else:
                done += [same_core[c], cross[c]]

        def pieces(masks, count):
            return [shape((count, height, lanes), BF16 if mask else F32) for mask in masks]

        def term(places, outs):
            return call(
                functools.partial(term_body, len(done), len(late), places, groups, skipped),
                outs,
                consts, weights, *begun, *done, *late,
                flops=2 * height * groups * 2 * slots * lanes * columns * lanes,
                scratch_shapes=[pltpu.VMEM((height, (2 * slots - skipped) * lanes), BF16)],
            )

        if c < chunks - 1 and len(steps) == 2 and len(steps[0]) == 4:
            (near, far, side, _), (last, _) = steps
            places = {near ^ last: (0, 0), near: (0, 1), far ^ last: (1, 0), far: (2, 0), side ^ last: (3, 0), side: (3, 1), last: (4, 0), 0: (4, 1)}
            sizes = ((2, BF16), (1, BF16), (1, F32), (2, BF16), (2, F32))
            to_near, to_last, to_far, to_side, keep = term(places, [shape((count, height, lanes), kind) for count, kind in sizes])
            got_near = exchange(to_near, 2 * near, 0)
            (to_far,) = call(functools.partial(add_body, 1), [shape((1, height, lanes), BF16)], to_far, exchange(to_last, 2 * last, 0))
            got_far = exchange(to_far, 2 * far, 0)
            got_side = exchange(to_side, 2 * side, 0)
            send, keep = call(functools.partial(add_body, 2), [shape((1, height, lanes), kind) for kind in (BF16, F32)], keep, got_near, got_side)
            keeps.append(keep)
            received.append([exchange(send, 2 * last, 0), got_far])
            continue

        outs = term(block_places(steps, cuts), [piece for start, stop in cuts for piece in pieces(steps[0], stop - start)])
        size = len(steps[0])
        state = [(outs[p * size:(p + 1) * size - 1], outs[(p + 1) * size - 1]) for p in range(len(cuts))]
        for at, masks in enumerate(steps):
            gots = [[exchange(sends[i], 2 * masks[i], 0) for i in range(len(sends))] for sends, _ in state]
            if at + 1 == len(steps):
                break
            after = steps[at + 1]
            count //= len(after)
            outs = []
            for p, (_, keep) in enumerate(state):
                start, stop = (cut // count for cut in cuts[p])
                outs += call(functools.partial(add_body, len(gots[p])), pieces(after[start:stop], count), keep, *gots[p])
            cuts = [(0, count)]
            state = [(outs[:-1], outs[-1])]
        keeps.append(state[0][1])
        received.append(gots[0])

    base = call(base_body, shape((own_tiles, rows, lanes), F32), hamiltonian, panel_tiles)
    finished = []
    done_piece = [shape((part, rows, lanes), BF16)] * 2
    for c in range(chunks - 1):
        finished += call(functools.partial(finish_body, c), done_piece, consts, base, keeps[c], *received[c])
    given = [consts, base, keeps[-1], *finished, *received[-1]]
    new_rows, new_sigma = call(
        functools.partial(last_body, chunks - 1),
        [shape((own_tiles, rows, lanes), BF16)] * 2,
        *given,
        in_specs=[vmem] * len(given),
        out_specs=[pl.BlockSpec(memory_space=pl.ANY)] * 2,
        scratch_shapes=[pltpu.VMEM((part, rows, lanes), BF16)] * 2 + [pltpu.SemaphoreType.DMA((2 * chunks,))],
    )
    return new_rows.reshape(panel_rows.shape), new_sigma.reshape(panel_rows.shape)


def solution(mesh):
    in_specs = (
        P("mem", "hist", None, None),
        P(("mem", "hist"), None, None),
        P(("hist", "mem"), None, None),
        P(),
        P(),
        P(),
        P(),
        P(),
    )
    out_specs = (P(("hist", "mem"), None, None), P(("hist", "mem"), None, None))
    return jax.shard_map(local, mesh=mesh, in_specs=in_specs, out_specs=out_specs, check_vma=False)
```
